32 devices in a mesh: groups: 2 (over x), path: 16 (over z, y, core).
Axes of the slice: x: 2, y: 2, z: 4, core: 2. Of those that a mesh axis runs over, the one named last changes fastest.
Arguments:
- path_angle: float32 [64, 8192], P(None, ('groups', 'path')), parts along dimension 1, may hold values from -3.140625 to 3.140625
- path_delay: float32 [64, 8192], P(None, ('groups', 'path')), parts along dimension 1, may hold values from 0 to 64
- path_gain: float32 [2, 64, 8192], P(None, None, ('groups', 'path')), parts along dimension 2, may hold values from -0.1 to 0.1
- material_ids: int32 [64, 8192], P(None, ('groups', 'path')), parts along dimension 1, may hold values from 0 to 15
- reflection: float32 [2, 16], replicated, may hold values from -1 to 1
- step_sizes: float32 [4], replicated, may hold values from 0.0005 to 0.002
- tone_ids: int32 [128], P('groups'), parts along dimension 0, may hold values from 0 to 3275
- symbol_ids: int32 [128, 64], P(('groups', 'path')), parts along dimension 0, may hold values from 0 to 15
- receiver_noise: float32 [128, 2, 256], P(('groups', 'path')), parts along dimension 0, may hold values from -2.4 to 2.4
Outputs:
- path_grad: float32 [2, 64, 8192], P(None, None, ('groups', 'path')), parts along dimension 2
- estimates: float32 [128, 2, 64], P(('groups', 'path')), parts along dimension 0
- material_grad: float32 [2, 32], P(None, 'groups'), parts along dimension 1
- channel: float32 [128, 2, 64, 256], P(('groups', 'path')), parts along dimension 0
The draws below stay inside these ranges and needn't reach their ends.
There are 2 independent parts, one for each index of `groups`. The reference program is written for one: setup_inputs(seed, part) draws one part's arguments, and reference() takes and returns one part's arrays. A program takes and returns all parts, laid end to end along the dimension named above; an argument that names none is the same for every part. Nothing has to cross between parts.
All inputs are finite; a program needn't handle non-finite values.
Results may differ from the reference program's by a relative error of at most 0.0003.
Values sent between devices are 32-bit elements; how exact they have to be, the bound alone decides.
No kernel may reach another device: no remote copies, remote signals or barrier semaphores. Data moves between devices by JAX's collectives and lax.ppermute only.
A program may use at most 128 MiB of HBM per device.

```python
import math
import jax
import jax.numpy as jnp
from jax import lax

U = 64
A = 256
MAT = 16
TONE_SPAN = 3276
LAYERS = 4
PU_DEV = 256
TONES = 64
PUS = 4096
N_PATH = 16


def set_ends(drawn, stream_key, smallest, largest):
    index_at = [jax.random.randint(jax.random.fold_in(stream_key, axis), (), 0, length) for axis, length in enumerate(drawn.shape)]
    widest = drawn.shape.index(max(drawn.shape))
    neighbour = index_at[:widest] + [(index_at[widest] + 1) % drawn.shape[widest]] + index_at[widest + 1:]
    return drawn.at[tuple(index_at)].set(smallest).at[tuple(neighbour)].set(largest)


def block_scale(stream_key, shape, cuts, low, high):
    factor_of = 1.0
    for position, blocks in cuts:
        draws = jax.random.uniform(jax.random.fold_in(jax.random.fold_in(stream_key, 6), position), (blocks,), jnp.float32, low / len(cuts), high / len(cuts))
        factor_of = factor_of * jnp.repeat(jnp.exp(draws), shape[position] // blocks).reshape((-1,) + (1,) * (len(shape) - 1 - position))
    return factor_of


def centred(key, extent, scale, limit, shards=(), kind=jnp.bfloat16):
    level = block_scale(key, extent, shards, -0.22, 0.18) if shards else 1.0
    result = jax.random.normal(key, extent, jnp.float32) * scale * level
    return jnp.minimum(jnp.maximum(result, -limit), limit).astype(kind)


def setup_inputs(seed: int = 0, part: int = 0) -> dict:
    key_list = jax.random.split(jax.random.key(seed), 10)
    own_keys = jax.random.split(jax.random.fold_in(key_list[9], part), 10)
    return {
        "path_angle": jnp.clip(jax.random.uniform(own_keys[0], (U, PUS), jnp.float32, -3.140625, 3.140625), -3.140625, 3.140625),
        "path_delay": jnp.clip(64.0 * jax.random.uniform(own_keys[1], (U, PUS), jnp.float32) ** block_scale(own_keys[1], (U, PUS), ((1, 16),), -0.2, 0.2), 0.0, 64.0),
        "path_gain": centred(own_keys[2], (2, U, PUS), ((PU_DEV * N_PATH) ** -0.5), 0.1, ((2, 16),), jnp.float32),
        "material_ids": set_ends(jax.random.randint(own_keys[3], (U, PUS), 0, MAT), jax.random.fold_in(own_keys[3], 1), 0, MAT - 1).astype(jnp.int32),
        "reflection": jnp.clip(jax.random.uniform(key_list[4], (2, MAT), jnp.float32, -1.0, 1.0), -1.0, 1.0),
        "step_sizes": jnp.clip(jnp.exp(jax.random.uniform(key_list[5], (LAYERS,), jnp.float32, math.log(0.0005), math.log(0.002))), 0.0005, 0.002),
        "tone_ids": set_ends(jax.random.randint(own_keys[6], (TONES,), 0, TONE_SPAN), jax.random.fold_in(own_keys[6], 1), 0, TONE_SPAN - 1).astype(jnp.int32),
        "symbol_ids": set_ends(jax.random.randint(own_keys[7], (TONES, U), 0, 16), jax.random.fold_in(own_keys[7], 1), 0, 15).astype(jnp.int32),
        "receiver_noise": centred(own_keys[8], (TONES, 2, A), 0.3, 2.4, ((0, 16),), jnp.float32),
    }


highest_mode = lax.Precision.HIGHEST
clip_level = 1.5
qam_scale = 1.0 / math.sqrt(10.0)
user_block = 8

def steering_block(angles):
    antenna_pos = jnp.arange(A, dtype=jnp.float32)
    spread = (math.pi * jnp.sin(angles))[..., None] * antenna_pos
    return (jnp.cos(spread), jnp.sin(spread))

def phase_block(tone_rows, delays):
    grid = (tone_rows.astype(jnp.float32) * (2.0 * math.pi / TONE_SPAN))[:, None, None] * delays[None]
    return (jnp.cos(grid), jnp.sin(grid))

def material_table(material_ids):
    return (material_ids[None] == jnp.arange(MAT, dtype=jnp.int32)[:, None, None]).astype(jnp.float32)

def coefficients(path_gain, picker, reflection):
    refl_real = lax.optimization_barrier(jnp.sum(reflection[0][:, None, None] * picker, 0))
    refl_imag = lax.optimization_barrier(jnp.sum(reflection[1][:, None, None] * picker, 0))
    coef_real = path_gain[0] * refl_real - path_gain[1] * refl_imag
    coef_imag = path_gain[0] * refl_imag + path_gain[1] * refl_real
    return (coef_real, coef_imag)

def split_users(field):
    return field.reshape((U // user_block, user_block) + field.shape[1:])

def synth_users(tone_rows, angles, delays, coef_real, coef_imag):
    row_count = tone_rows.shape[0]

    def one_block(items):
        ang, dly, c_real, c_imag = items
        s_cos, s_sin = steering_block(ang)
        p_cos, p_sin = phase_block(tone_rows, dly)
        g_real = c_real[None] * p_cos + c_imag[None] * p_sin
        g_imag = c_imag[None] * p_cos - c_real[None] * p_sin
        form = 'fbp,bpa->fba'
        h_real = jnp.einsum(form, g_real, s_cos, precision=highest_mode) + jnp.einsum(form, g_imag, s_sin, precision=highest_mode)
        h_imag = jnp.einsum(form, g_imag, s_cos, precision=highest_mode) - jnp.einsum(form, g_real, s_sin, precision=highest_mode)
        return jnp.stack([h_real, h_imag], 1)
    blocks = lax.map(one_block, (split_users(angles), split_users(delays), split_users(coef_real), split_users(coef_imag)))
    return jnp.transpose(blocks, (1, 2, 0, 3, 4)).reshape(row_count, 2, U, A)

def grad_users(tone_rows, channel_grads, angles, delays):
    row_count = channel_grads.shape[0]
    grad_real = jnp.transpose(channel_grads[:, 0].reshape(row_count, U // user_block, user_block, A), (1, 0, 2, 3))
    grad_imag = jnp.transpose(channel_grads[:, 1].reshape(row_count, U // user_block, user_block, A), (1, 0, 2, 3))

    def one_block(items):
        ang, dly, g_real, g_imag = items
        s_cos, s_sin = steering_block(ang)
        form = 'fba,bpa->fbp'
        q_real = jnp.einsum(form, g_real, s_cos, precision=highest_mode) - jnp.einsum(form, g_imag, s_sin, precision=highest_mode)
        q_imag = jnp.einsum(form, g_real, s_sin, precision=highest_mode) + jnp.einsum(form, g_imag, s_cos, precision=highest_mode)
        p_cos, p_sin = phase_block(tone_rows, dly)
        term_real = lax.optimization_barrier(jnp.sum(p_cos * q_real - p_sin * q_imag, 0))
        term_imag = lax.optimization_barrier(jnp.sum(p_cos * q_imag + p_sin * q_real, 0))
        return jnp.stack([term_real, term_imag])
    blocks = lax.map(one_block, (split_users(angles), split_users(delays), grad_real, grad_imag))
    return jnp.transpose(blocks, (1, 0, 2, 3)).reshape(2, U, angles.shape[1])

def detector_loss(responses, symbol_ids, receiver_noise, step_sizes):
    sym_real = (2 * (symbol_ids % 4) - 3).astype(jnp.float32) * qam_scale
    sym_imag = (2 * (symbol_ids // 4) - 3).astype(jnp.float32) * qam_scale
    chan_real = responses[:, 0]
    chan_imag = responses[:, 1]

    def forward_mix(channel, vector):
        return jnp.einsum('fua,fu->fa', channel, vector, precision=highest_mode)

    def adjoint_mix(channel, vector):
        return jnp.einsum('fua,fa->fu', channel, vector, precision=highest_mode)
    obs_real = forward_mix(chan_real, sym_real) - forward_mix(chan_imag, sym_imag) + receiver_noise[:, 0]
    obs_imag = forward_mix(chan_real, sym_imag) + forward_mix(chan_imag, sym_real) + receiver_noise[:, 1]
    est_real = jnp.zeros_like(sym_real)
    est_imag = jnp.zeros_like(sym_imag)
    for layer_index in range(LAYERS):
        err_real = obs_real - (forward_mix(chan_real, est_real) - forward_mix(chan_imag, est_imag))
        err_imag = obs_imag - (forward_mix(chan_real, est_imag) + forward_mix(chan_imag, est_real))
        step_real = adjoint_mix(chan_real, err_real) + adjoint_mix(chan_imag, err_imag)
        step_imag = adjoint_mix(chan_real, err_imag) - adjoint_mix(chan_imag, err_real)
        est_real = clip_level * jnp.tanh((est_real + step_sizes[layer_index] * step_real) / clip_level)
        est_imag = clip_level * jnp.tanh((est_imag + step_sizes[layer_index] * step_imag) / clip_level)
    loss_value = jnp.sum((est_real - sym_real) ** 2 + (est_imag - sym_imag) ** 2) / U
    return (loss_value, jnp.stack([est_real, est_imag], 1))

def detector_grads(responses, symbol_ids, receiver_noise, step_sizes):

    def wrapped(channel):
        return detector_loss(channel, symbol_ids, receiver_noise, step_sizes)
    loss_value, pullback, estimates = jax.vjp(wrapped, responses, has_aux=True)
    return (pullback(jnp.ones_like(loss_value))[0], estimates)

def material_terms(path_gain, path_grad, picker):
    along_real = path_gain[0] * path_grad[0] + path_gain[1] * path_grad[1]
    along_imag = path_gain[0] * path_grad[1] - path_gain[1] * path_grad[0]
    return jnp.stack([lax.optimization_barrier(jnp.sum(picker * along_real[None], (1, 2))), lax.optimization_barrier(jnp.sum(picker * along_imag[None], (1, 2)))])

def reference(path_angle, path_delay, path_gain, material_ids, reflection, step_sizes, tone_ids, symbol_ids, receiver_noise):
    picker = material_table(material_ids)
    coef_real, coef_imag = coefficients(path_gain, picker, reflection)
    responses = synth_users(tone_ids, path_angle, path_delay, coef_real, coef_imag)
    channel_grads, estimates = detector_grads(responses, symbol_ids, receiver_noise, step_sizes)
    path_grad = grad_users(tone_ids, channel_grads, path_angle, path_delay)
    material_grad = material_terms(path_gain, path_grad, picker)
    return (path_grad, estimates, material_grad, responses)
```

```python
import functools
import math

import jax
import jax.numpy as jnp
from jax import lax
from jax.experimental import pallas as pl
from jax.experimental.pallas import tpu as pltpu
from jax.sharding import PartitionSpec as P

MAT = 16
TONE_SPAN = 3276
LAYERS = 4
FIELDS = 5

clip_level = 1.5
qam_scale = 1.0 / math.sqrt(10.0)

SINE = (
    6.283185160088971,
    -41.341655031286386,
    81.60100406453228,
    -76.5497820808334,
    39.536704364112744,
)


def cos_turns(t):
    a = 0.25 - jnp.abs(t - jnp.round(t))
    z = a * a
    p = SINE[4] * z + SINE[3]
    p = p * z + SINE[2]
    p = p * z + SINE[1]
    p = p * z + SINE[0]
    return p * a


def swap_halves(x):
    return pltpu.roll(x, 4, x.ndim - 2)


def half_rows(shape, dim, top, bottom):
    row = lax.broadcasted_iota(jnp.int32, shape, dim)
    return jnp.where(row % 8 < 4, jnp.float32(top), jnp.float32(bottom))


def top_mask(shape, dim):
    return lax.broadcasted_iota(jnp.int32, shape, dim) % 8 < 4


def split(x):
    high = x.astype(jnp.bfloat16)
    low = (x - high.astype(jnp.float32)).astype(jnp.bfloat16)
    return high, low


def synth_kernel(n, ul, refl_ref, x_ref, tone_ref, h_ref, w_ref, e_ref, lhs_ref, acc_ref):
    u = pl.program_id(0)
    pw = x_ref.shape[-1]
    half = w_ref.shape[-2] // 4
    rows = acc_ref.shape[0]
    top8 = top_mask((8, pw), 0)
    shift8 = half_rows((8, pw), 0, 0.0, -0.25)
    fine_row = lax.broadcasted_iota(jnp.int32, (32, pw), 0)
    fine_coef = (fine_row % 16).astype(jnp.float32) + 0.5
    fine_shift = jnp.where(fine_row < 16, 0.0, -0.25)
    blocks = half // 16
    coarse_row = lax.broadcasted_iota(jnp.int32, (2 * blocks, pw), 0)
    coarse_coef = (coarse_row % blocks).astype(jnp.float32) * 16.0
    coarse_shift = jnp.where(coarse_row < blocks, 0.0, -0.25)

    acc_ref[...] = jnp.zeros_like(acc_ref)

    def tile(s, carry):
        def row(j):
            return x_ref[s, pl.ds(j * ul + u, 1), :]

        w, dly, g_re, g_im, mat = (row(j) for j in range(FIELDS))
        wide = jnp.broadcast_to(w, (8, pw))
        w32 = jnp.concatenate([wide] * 4, 0)
        fine = cos_turns(fine_coef * w32 + fine_shift)
        w16 = jnp.concatenate([wide] * (2 * blocks // 8), 0)
        coarse = cos_turns(coarse_coef * w16 + coarse_shift)
        f_cos, f_sin = fine[:16], fine[16:]
        for b in range(blocks):
            c_cos = coarse[b : b + 1]
            c_sin = coarse[blocks + b : blocks + b + 1]
            a_cos = c_cos * f_cos - c_sin * f_sin
            a_sin = c_sin * f_cos + c_cos * f_sin
            for base, val in ((0, a_cos), (half, a_sin)):
                high, low = split(val)
                w_ref[0, s, pl.ds(base + 16 * b, 16), :] = high
                w_ref[0, s, pl.ds(2 * half + base + 16 * b, 16), :] = low
        mat8 = jnp.broadcast_to(mat, (8, pw))
        r_re = jnp.zeros((8, pw), jnp.float32)
        r_im = jnp.zeros((8, pw), jnp.float32)
        for m in range(MAT):
            hit = mat8 == float(m)
            r_re = jnp.where(hit, refl_ref[0, m], r_re)
            r_im = jnp.where(hit, refl_ref[1, m], r_im)
        c_re = g_re * r_re - g_im * r_im
        c_im = g_re * r_im + g_im * r_re
        c_mix = jnp.where(top8, c_re, -c_re)
        centre = w * (half - 0.5)
        centre = centre - jnp.round(centre)
        base8 = shift8 + centre
        d8 = jnp.broadcast_to(dly, (8, pw))
        step = 32
        for q in range(rows // step):
            rq = pl.ds(q * step, step)
            tone = tone_ref[rq, :]
            tone = jnp.concatenate([tone] * (pw // 128), 1)
            d32 = jnp.concatenate([d8] * (step // 8), 0)
            b32 = jnp.concatenate([base8] * (step // 8), 0)
            e = cos_turns(tone * d32 + b32)
            e_ref[0, s, rq, :] = e
            e3 = e.reshape(step // 8, 8, pw)
            g = e3 * c_mix[None] + swap_halves(e3) * c_im[None]
            high, low = split(g.reshape(step, pw))
            lhs_ref[rq, pl.ds(0, pw)] = high
            lhs_ref[rq, pl.ds(pw, pw)] = low
        dims = (((1,), (1,)), ((), ()))
        w_high = w_ref[0, s, pl.ds(0, 2 * half), :]
        w_low = w_ref[0, s, pl.ds(2 * half, 2 * half), :]
        l_high = lhs_ref[:, pl.ds(0, pw)]
        left = jnp.concatenate([lhs_ref[...], l_high], 1)
        right = jnp.concatenate([w_high, w_high, w_low], 1)
        acc_ref[...] += lax.dot_general(left, right, dims, preferred_element_type=jnp.float32)
        return carry

    lax.fori_loop(0, n, tile, 0)
    even = acc_ref[:, pl.ds(0, half)].reshape(rows // 8, 8, half)
    odd = acc_ref[:, pl.ds(half, half)].reshape(rows // 8, 8, half)
    odd = swap_halves(odd) * half_rows(odd.shape, 1, 1.0, -1.0)
    h_ref[:, 0, :, pl.ds(0, half)] = even + odd
    h_ref[:, 0, :, pl.ds(half, half)] = even - odd


def synthesize(params, tone_rows, reflection, antennas):
    n, wide, pw = params.shape
    ul = wide // FIELDS
    rows = tone_rows.shape[0]
    return pl.pallas_call(
        functools.partial(synth_kernel, n, ul),
        grid=(ul,),
        in_specs=[
            pl.BlockSpec(memory_space=pltpu.SMEM),
            pl.BlockSpec((n, wide, pw), lambda u: (0, 0, 0)),
            pl.BlockSpec((rows, 128), lambda u: (0, 0)),
        ],
        out_specs=[
            pl.BlockSpec((n, 1, 8, antennas), lambda u: (0, u, 0, 0)),
            pl.BlockSpec((1, n, 2 * antennas, pw), lambda u: (u, 0, 0, 0)),
            pl.BlockSpec((1, n, rows, pw), lambda u: (u, 0, 0, 0)),
        ],
        out_shape=[
            jax.ShapeDtypeStruct((n, ul, 8, antennas), jnp.float32),
            jax.ShapeDtypeStruct((ul, n, 2 * antennas, pw), jnp.bfloat16),
            jax.ShapeDtypeStruct((ul, n, rows, pw), jnp.float32),
        ],
        scratch_shapes=[
            pltpu.VMEM((rows, 2 * pw), jnp.bfloat16),
            pltpu.VMEM((rows, antennas), jnp.float32),
        ],
        compiler_params=pltpu.CompilerParams(vmem_limit_bytes=48 << 20),
        name="synth",
    )(reflection, params, tone_rows)


def detect_kernel(users, h_ref, s_ref, n_ref, step_ref, g_ref, x_out_ref, xs_ref, gz_ref, gx_ref):
    ant = h_ref.shape[-1]
    tiles = ant // 128
    top = top_mask((8, 128), 0)
    top_a = top_mask((8, ant), 0)
    chunk = 8

    def wide(x):
        return jnp.concatenate([x] * tiles, 1) if tiles > 1 else x

    def forward(get):
        def body(i, c):
            a, b = c
            for k in range(chunk):
                u = i * chunk + k
                h = h_ref[u]
                x = get(u)
                a = a + h * wide(x)
                b = b + h * wide(swap_halves(x))
            return a, b

        zero = jnp.zeros((8, ant), jnp.float32)
        a, b = lax.fori_loop(0, users // chunk, body, (zero, zero))
        return jnp.where(top_a, a - swap_halves(a), b + swap_halves(b))

    def adjoint(e, put):
        es = swap_halves(e)

        def body(i, c):
            for k in range(chunk):
                u = i * chunk + k
                h = h_ref[u]
                m, q = h * e, h * es
                m = sum(m[:, 128 * t : 128 * t + 128] for t in range(tiles))
                q = sum(q[:, 128 * t : 128 * t + 128] for t in range(tiles))
                v = jnp.where(top, m + swap_halves(m), swap_halves(q) - q)
                put(u, jnp.broadcast_to(jnp.sum(v, 1, keepdims=True), (8, 128)))
            return c

        lax.fori_loop(0, users // chunk, body, 0)

    y = forward(lambda u: s_ref[u]) + n_ref[...]
    errs = []
    for layer in range(LAYERS):
        e = y if layer == 0 else y - forward(lambda u: xs_ref[layer, u])
        errs.append(e)
        step = step_ref[layer]

        def put(u, v):
            z = step * v if layer == 0 else xs_ref[layer, u] + step * v
            xs_ref[layer + 1, u] = clip_level * jnp.tanh(z * (1.0 / clip_level))

        adjoint(e, put)

    x_out_ref[...] = xs_ref[LAYERS]
    backs = [None] * LAYERS
    for layer in reversed(range(LAYERS)):
        step = step_ref[layer]
        last = layer == LAYERS - 1

        def slope(i, c):
            for k in range(chunk):
                u = i * chunk + k
                x = xs_ref[layer + 1, u]
                gx = (x - s_ref[u]) * (2.0 / users) if last else gx_ref[u]
                t = x * (1.0 / clip_level)
                gz_ref[layer, u] = gx * (1.0 - t * t) * step
            return c

        lax.fori_loop(0, users // chunk, slope, 0)
        ge = forward(lambda u: gz_ref[layer, u])
        backs[layer] = ge
        if layer:
            inv = None

            def put(u, v):
                x = xs_ref[layer + 1, u]
                gx = (x - s_ref[u]) * (2.0 / users) if last else gx_ref[u]
                t = x * (1.0 / clip_level)
                gx_ref[u] = gx * (1.0 - t * t) - v

            adjoint(ge, put)

    sign = half_rows((8, ant), 0, 1.0, -1.0)
    pairs = [(v, sign * swap_halves(v)) for k in range(LAYERS) for v in (errs[k], backs[k])]

    def body(u, c):
        s = s_ref[u]
        g = jnp.zeros((8, ant), jnp.float32)
        for k in range(LAYERS):
            for which in range(2):
                v, vs = pairs[2 * k + which]
                if which == 0:
                    b = gz_ref[k, u]
                else:
                    b = s - xs_ref[k, u] if k else s
                bs = swap_halves(b)
                g = g + v * wide(jnp.where(top, b, bs)) + vs * wide(jnp.where(top, bs, b))
        g_ref[u] = g
        return c

    lax.fori_loop(0, users, body, 0)


def detect(channel, symbols, noise, step_sizes):
    users, _, ant = channel.shape
    return pl.pallas_call(
        functools.partial(detect_kernel, users),
        in_specs=[
            pl.BlockSpec(memory_space=pltpu.VMEM),
            pl.BlockSpec(memory_space=pltpu.VMEM),
            pl.BlockSpec(memory_space=pltpu.VMEM),
            pl.BlockSpec(memory_space=pltpu.SMEM),
        ],
        out_specs=[pl.BlockSpec(memory_space=pltpu.VMEM), pl.BlockSpec(memory_space=pltpu.VMEM)],
        out_shape=[
            jax.ShapeDtypeStruct((users, 8, ant), jnp.float32),
            jax.ShapeDtypeStruct((users, 8, 128), jnp.float32),
        ],
        scratch_shapes=[
            pltpu.VMEM((LAYERS + 1, users, 8, 128), jnp.float32),
            pltpu.VMEM((LAYERS, users, 8, 128), jnp.float32),
            pltpu.VMEM((users, 8, 128), jnp.float32),
        ],
        compiler_params=pltpu.CompilerParams(vmem_limit_bytes=16 << 20),
        name="detect",
    )(channel, symbols, noise, step_sizes)


def grad_kernel(n, ul, parts, g_ref, w_ref, e_ref, x_ref, out_ref, lhs_ref, mat_ref):
    u = pl.program_id(0)
    part = pl.program_id(1)
    pw = x_ref.shape[-1]
    ant = g_ref.shape[-1]
    half = ant // 2
    rows = lhs_ref.shape[0]

    @pl.when(part == 0)
    def _():
        plus = g_ref[:, 0, :, pl.ds(0, half)]
        minus = g_ref[:, 0, :, pl.ds(half, half)]
        odd = swap_halves(plus - minus) * half_rows(plus.shape, 1, -1.0, 1.0)
        mix = jnp.concatenate([plus + minus, odd], 2).reshape(rows, ant)
        high, low = split(mix)
        lhs_ref[:, pl.ds(0, ant)] = high
        lhs_ref[:, pl.ds(ant, ant)] = low

    @pl.when((part == 0) & (u == 0))
    def _():
        mat_ref[...] = jnp.zeros_like(mat_ref)

    sign = half_rows((8, pw), 0, 1.0, -1.0)
    kinds = lax.broadcasted_iota(jnp.int32, (MAT, pw), 0).astype(jnp.float32)
    per = n // parts

    def tile(i, carry):
        s = part * per + i
        w_high = w_ref[0, i, pl.ds(0, ant), :]
        w_low = w_ref[0, i, pl.ds(ant, ant), :]
        left = jnp.concatenate([lhs_ref[...], lhs_ref[:, pl.ds(0, ant)]], 1)
        right = jnp.concatenate([w_high, w_high, w_low], 0)
        q = jnp.dot(left, right, preferred_element_type=jnp.float32).reshape(rows // 8, 8, pw)
        e = e_ref[0, i].reshape(rows // 8, 8, pw)
        a = jnp.sum(e * q, 0)
        b = jnp.sum(swap_halves(e) * q, 0)
        p_re = jnp.sum(a * sign, 0, keepdims=True)
        p_im = jnp.sum(b, 0, keepdims=True)
        out_ref[s, pl.ds(u, 1), :] = p_re
        out_ref[s, pl.ds(ul + u, 1), :] = p_im

        def row(j):
            return x_ref[s, pl.ds(j * ul + u, 1), :]

        g_re, g_im, mat = row(2), row(3), row(4)
        along_re = g_re * p_re + g_im * p_im
        along_im = g_re * p_im - g_im * p_re
        hit = jnp.broadcast_to(mat, (MAT, pw)) == kinds
        mat_ref[0] += jnp.where(hit, jnp.broadcast_to(along_re, (MAT, pw)), 0.0)
        mat_ref[1] += jnp.where(hit, jnp.broadcast_to(along_im, (MAT, pw)), 0.0)
        return carry

    lax.fori_loop(0, per, tile, 0)

    @pl.when((u == ul - 1) & (part == parts - 1))
    def _():
        lane = lax.broadcasted_iota(jnp.int32, (MAT, pw), 1)
        kind = lax.broadcasted_iota(jnp.int32, (MAT, pw), 0)
        line = jnp.zeros((1, pw), jnp.float32)
        for j in range(2):
            total = jnp.sum(mat_ref[j], 1, keepdims=True)
            spread = jnp.where(lane == kind + j * MAT, jnp.broadcast_to(total, (MAT, pw)), 0.0)
            line = line + jnp.sum(spread, 0, keepdims=True)
        for s in range(n):
            out_ref[s, pl.ds(2 * ul, 1), :] = line


def gradient(grads, steer, tones, params):
    n, ul, _, ant = grads.shape
    wide, pw = params.shape[1:]
    rows = tones.shape[2]
    parts = 4 if n % 4 == 0 else 1
    per = n // parts
    return pl.pallas_call(
        functools.partial(grad_kernel, n, ul, parts),
        grid=(ul, parts),
        in_specs=[
            pl.BlockSpec((n, 1, 8, ant), lambda u, j: (0, u, 0, 0)),
            pl.BlockSpec((1, per, 2 * ant, pw), lambda u, j: (u, j, 0, 0)),
            pl.BlockSpec((1, per, rows, pw), lambda u, j: (u, j, 0, 0)),
            pl.BlockSpec((n, wide, pw), lambda u, j: (0, 0, 0)),
        ],
        out_specs=pl.BlockSpec((n, 2 * ul + 1, pw), lambda u, j: (0, 0, 0)),
        out_shape=jax.ShapeDtypeStruct((n, 2 * ul + 1, pw), jnp.float32),
        scratch_shapes=[
            pltpu.VMEM((rows, 2 * ant), jnp.bfloat16),
            pltpu.VMEM((2, MAT, pw), jnp.float32),
        ],
        compiler_params=pltpu.CompilerParams(vmem_limit_bytes=32 << 20),
        name="gradient",
    )(grads, steer, tones, params)


def exchange(x):
    return lax.all_to_all(x, "path", 0, 0, tiled=True)


def local(
    n,
    path_angle,
    path_delay,
    path_gain,
    material_ids,
    reflection,
    step_sizes,
    tone_ids,
    symbol_ids,
    receiver_noise,
):
    users, pw = path_angle.shape
    own, _, ant = receiver_noise.shape
    assert 2 * own == 8
    half = ant // 2
    ul = users // n
    fields = (
        0.5 * jnp.sin(path_angle),
        path_delay,
        path_gain[0],
        path_gain[1],
        material_ids.astype(jnp.float32),
    )
    params = exchange(jnp.concatenate([f.reshape(n, ul, pw) for f in fields], 1))
    tone = tone_ids.astype(jnp.float32) * (1.0 / TONE_SPAN)
    tone = jnp.broadcast_to(tone.reshape(n, 1, own, 1), (n, 2, own, 128)).reshape(8 * n, 128)
    channel_rows, steer, tones = synthesize(params, tone, reflection, ant)
    channel = exchange(channel_rows).reshape(users, 8, ant)

    symbols = jnp.stack([symbol_ids % 4, symbol_ids // 4], 0)
    symbols = (2 * symbols - 3).astype(jnp.float32) * qam_scale
    symbols = jnp.transpose(symbols, (2, 0, 1)).reshape(users, 8, 1)
    symbols = jnp.broadcast_to(symbols, (users, 8, 128))
    noise = jnp.transpose(receiver_noise, (1, 0, 2)).reshape(8, ant)
    noise = jnp.concatenate([noise[:, half:], noise[:, :half][:, ::-1]], 1)
    grads, found = detect(channel, symbols, noise, step_sizes)
    estimates = jnp.transpose(found[:, :, 0].reshape(users, 2, own), (2, 1, 0))

    grads = exchange(grads.reshape(n, ul, 8, ant))
    sent = gradient(grads, steer, tones, params)
    back = exchange(sent)
    path_grad = jnp.transpose(back[:, : 2 * ul].reshape(n, 2, ul, pw), (1, 0, 2, 3))
    path_grad = path_grad.reshape(2, users, pw)
    material_grad = jnp.sum(back[:, 2 * ul, : 2 * MAT], 0).reshape(2, MAT)

    responses = jnp.transpose(channel.reshape(users, 2, own, ant), (2, 1, 0, 3))
    responses = jnp.concatenate([responses[..., half:][..., ::-1], responses[..., :half]], -1)
    return (path_grad, estimates, material_grad, responses)


def solution(mesh):
    in_specs = (
        P(None, ("groups", "path")),
        P(None, ("groups", "path")),
        P(None, None, ("groups", "path")),
        P(None, ("groups", "path")),
        P(),
        P(),
        P("groups"),
        P(("groups", "path"), None),
        P(("groups", "path"), None, None),
    )
    out_specs = (
        P(None, None, ("groups", "path")),
        P(("groups", "path"), None, None),
        P(None, "groups"),
        P(("groups", "path"), None, None, None),
    )
    body = functools.partial(local, mesh.shape["path"])
    return jax.shard_map(body, mesh=mesh, in_specs=in_specs, out_specs=out_specs, check_vma=False)
```

```python
import functools
import math

import jax
import jax.numpy as jnp
from jax import lax
from jax.experimental import pallas as pl
from jax.experimental.pallas import tpu as pltpu
from jax.sharding import PartitionSpec as P

MAT = 16
TONE_SPAN = 3276
LAYERS = 4
FIELDS = 5

SYNTH_VMEM = 48 << 20
GRAD_VMEM = 48 << 20
SYNTH_UNROLL = 2
GRAD_UNROLL = 4
GRAD_STEPS = 2

clip_level = 1.5
qam_scale = 1.0 / math.sqrt(10.0)

SINE = (
    6.283185160088971,
    -41.341655031286386,
    81.60100406453228,
    -76.5497820808334,
    39.536704364112744,
)


def cos_turns(t):
    a = 0.25 - jnp.abs(t - jnp.round(t))
    z = a * a
    p = SINE[4] * z + SINE[3]
    p = p * z + SINE[2]
    p = p * z + SINE[1]
    p = p * z + SINE[0]
    return p * a


RISE = (
    -0.16666660462354993,
    0.00833308816681783,
    -0.00019811112712181806,
    2.6089325665533767e-06,
)


def sine(angle):
    t = jnp.abs(angle)
    y = jnp.where(t > 0.5 * math.pi, (3.140625 - t) + (math.pi - 3.140625), t)
    z = y * y
    p = RISE[3] * z + RISE[2]
    p = p * z + RISE[1]
    p = p * z + RISE[0]
    s = y + (y * z) * p
    return jnp.where(angle < 0.0, -s, s)


def swap_halves(x):
    return pltpu.roll(x, 4, x.ndim - 2)


def half_rows(shape, dim, top, bottom):
    row = lax.broadcasted_iota(jnp.int32, shape, dim)
    return jnp.where(row % 8 < 4, jnp.float32(top), jnp.float32(bottom))


def top_mask(shape, dim):
    return lax.broadcasted_iota(jnp.int32, shape, dim) % 8 < 4


def split(x):
    high = x.astype(jnp.bfloat16)
    low = (x - high.astype(jnp.float32)).astype(jnp.bfloat16)
    return high, low


def pack_kernel(n, ul, angle_ref, delay_ref, gain_ref, ids_ref, out_ref):
    pw = angle_ref.shape[-1]
    fields = (
        0.5 * sine(angle_ref[...]),
        delay_ref[...],
        gain_ref[0],
        gain_ref[1],
        ids_ref[...].astype(jnp.float32),
    )
    parts = pw // 128
    for j, field in enumerate(fields):
        for t in range(parts):
            block = field[:, 128 * t : 128 * t + 128]
            for d in range(n):
                start = (j * parts + t) * ul
                out_ref[d, pl.ds(start, ul), :] = block[d * ul : d * ul + ul]


def pack(n, angle, delay, gain, ids):
    users, pw = angle.shape
    ul = users // n
    rows = FIELDS * ul * (pw // 128)
    return pl.pallas_call(
        functools.partial(pack_kernel, n, ul),
        in_specs=[pl.BlockSpec(memory_space=pltpu.VMEM)] * 4,
        out_specs=pl.BlockSpec(memory_space=pltpu.VMEM),
        out_shape=jax.ShapeDtypeStruct((n, rows, 128), jnp.float32),
        compiler_params=pltpu.CompilerParams(vmem_limit_bytes=60 << 20),
        name="pack",
    )(angle, delay, gain, ids)


def field_row(x_ref, parts, ul, s, j, u):
    rows = [x_ref[s, pl.ds((j * parts + t) * ul + u, 1), :] for t in range(parts)]
    return jnp.concatenate(rows, 1)


def synth_kernel(n, ul, pw, unroll, x_ref, aux_ref, h_ref, w_ref, e_ref, lhs_ref, acc_ref):
    u = pl.program_id(0)
    parts = pw // 128
    half = w_ref.shape[-2] // 4
    rows = acc_ref.shape[0]
    top8 = top_mask((8, pw), 0)
    shift8 = half_rows((8, pw), 0, 0.0, -0.25)
    fine_row = lax.broadcasted_iota(jnp.int32, (32, pw), 0)
    fine_coef = (fine_row % 16).astype(jnp.float32) + 0.5
    fine_shift = jnp.where(fine_row < 16, 0.0, -0.25)
    blocks = half // 16
    coarse_row = lax.broadcasted_iota(jnp.int32, (2 * blocks, pw), 0)
    coarse_coef = (coarse_row % blocks).astype(jnp.float32) * 16.0
    coarse_shift = jnp.where(coarse_row < blocks, 0.0, -0.25)

    def wide(m):
        block = aux_ref[pl.ds(rows + 8 * m, 8), :]
        return jnp.concatenate([block] * parts, 1)

    def tile(s, carry):
        w, dly, g_re, g_im, mat = (field_row(x_ref, parts, ul, s, j, u) for j in range(FIELDS))
        w8 = jnp.broadcast_to(w, (8, pw))
        w32 = jnp.concatenate([w8] * 4, 0)
        fine = cos_turns(fine_coef * w32 + fine_shift)
        w16 = jnp.concatenate([w8] * (2 * blocks // 8), 0)
        coarse = cos_turns(coarse_coef * w16 + coarse_shift)
        f_cos, f_sin = fine[:16], fine[16:]
        for b in range(blocks):
            c_cos = coarse[b : b + 1]
            c_sin = coarse[blocks + b : blocks + b + 1]
            a_cos = c_cos * f_cos - c_sin * f_sin
            a_sin = c_sin * f_cos + c_cos * f_sin
            for base, val in ((0, a_cos), (half, a_sin)):
                high, low = split(val)
                w_ref[0, s, pl.ds(base + 16 * b, 16), :] = high
                w_ref[0, s, pl.ds(2 * half + base + 16 * b, 16), :] = low
        mat8 = jnp.broadcast_to(mat, (8, pw)).astype(jnp.int32)
        level = [wide(m) for m in range(MAT)]
        for bit in range(MAT.bit_length() - 1):
            hit = (mat8 & (1 << bit)) != 0
            level = [jnp.where(hit, y, x) for x, y in zip(level[::2], level[1::2])]
        refl = level[0]
        flip = swap_halves(refl)
        r_re, r_im = jnp.where(top8, refl, flip), jnp.where(top8, flip, refl)
        c_re = g_re * r_re - g_im * r_im
        c_im = g_re * r_im + g_im * r_re
        c_mix = jnp.where(top8, c_re, -c_re)
        centre = w * (half - 0.5)
        centre = centre - jnp.round(centre)
        base8 = shift8 + centre
        d8 = jnp.broadcast_to(dly, (8, pw))
        step = 32
        for q in range(rows // step):
            rq = pl.ds(q * step, step)
            tone = aux_ref[rq, :]
            tone = jnp.concatenate([tone] * parts, 1)
            d32 = jnp.concatenate([d8] * (step // 8), 0)
            b32 = jnp.concatenate([base8] * (step // 8), 0)
            e = cos_turns(tone * d32 + b32)
            e_ref[0, s, rq, :] = e
            e3 = e.reshape(step // 8, 8, pw)
            g = e3 * c_mix[None] + swap_halves(e3) * c_im[None]
            high, low = split(g.reshape(step, pw))
            lhs_ref[s % 2, rq, pl.ds(0, pw)] = high
            lhs_ref[s % 2, rq, pl.ds(pw, pw)] = low
        dims = (((1,), (1,)), ((), ()))
        w_high = w_ref[0, s, pl.ds(0, 2 * half), :]
        w_low = w_ref[0, s, pl.ds(2 * half, 2 * half), :]
        l_high = lhs_ref[s % 2, :, pl.ds(0, pw)]
        left = jnp.concatenate([l_high, lhs_ref[s % 2, :, pl.ds(pw, pw)]], 0)
        pair = lax.dot_general(left, w_high, dims, preferred_element_type=jnp.float32)
        rest = lax.dot_general(l_high, w_low, dims, preferred_element_type=jnp.float32)
        acc_ref[...] += pair[:rows] + (pair[rows:] + rest)
        return carry

    acc_ref[...] = jnp.zeros_like(acc_ref)
    lax.fori_loop(0, n, tile, 0, unroll=unroll)
    even = acc_ref[:, pl.ds(0, half)].reshape(rows // 8, 8, half)
    odd = acc_ref[:, pl.ds(half, half)].reshape(rows // 8, 8, half)
    odd = swap_halves(odd) * half_rows(odd.shape, 1, 1.0, -1.0)
    h_ref[:, 0, :, pl.ds(0, half)] = even + odd
    h_ref[:, 0, :, pl.ds(half, half)] = even - odd


def synthesize(params, aux, ul, pw, antennas):
    n, wide, _ = params.shape
    rows = 8 * n
    return pl.pallas_call(
        functools.partial(synth_kernel, n, ul, pw, min(n, SYNTH_UNROLL)),
        grid=(ul,),
        in_specs=[
            pl.BlockSpec((n, wide, 128), lambda u: (0, 0, 0)),
            pl.BlockSpec(aux.shape, lambda u: (0, 0)),
        ],
        out_specs=[
            pl.BlockSpec((n, 1, 8, antennas), lambda u: (0, u, 0, 0)),
            pl.BlockSpec((1, n, 2 * antennas, pw), lambda u: (u, 0, 0, 0)),
            pl.BlockSpec((1, n, rows, pw), lambda u: (u, 0, 0, 0)),
        ],
        out_shape=[
            jax.ShapeDtypeStruct((n, ul, 8, antennas), jnp.float32),
            jax.ShapeDtypeStruct((ul, n, 2 * antennas, pw), jnp.bfloat16),
            jax.ShapeDtypeStruct((ul, n, rows, pw), jnp.float32),
        ],
        scratch_shapes=[
            pltpu.VMEM((2, rows, 2 * pw), jnp.bfloat16),
            pltpu.VMEM((rows, antennas), jnp.float32),
        ],
        compiler_params=pltpu.CompilerParams(vmem_limit_bytes=SYNTH_VMEM),
        name="synth",
    )(params, aux)


def detect_kernel(users, h_ref, s_ref, n_ref, g_ref, x_out_ref, xs_ref, gz_ref, gx_ref):
    ant = h_ref.shape[-1]
    tiles = ant // 128
    top = top_mask((8, 128), 0)
    top_a = top_mask((8, ant), 0)
    chunk = 16

    def wide(x):
        return jnp.concatenate([x] * tiles, 1) if tiles > 1 else x

    def forward(get):
        def body(i, c):
            c = list(c)
            for k in range(chunk):
                u = i * chunk + k
                h = h_ref[u]
                x = get(u)
                j = 2 * (k % 4)
                c[j] = c[j] + h * wide(x)
                c[j + 1] = c[j + 1] + h * wide(swap_halves(x))
            return tuple(c)

        zero = jnp.zeros((8, ant), jnp.float32)
        c = lax.fori_loop(0, users // chunk, body, (zero,) * 8)
        a = (c[0] + c[2]) + (c[4] + c[6])
        b = (c[1] + c[3]) + (c[5] + c[7])
        return jnp.where(top_a, a - swap_halves(a), b + swap_halves(b))

    def adjoint(e, put):
        es = swap_halves(e)

        def body(i, c):
            for k in range(chunk):
                u = i * chunk + k
                h = h_ref[u]
                m, q = h * e, h * es
                m = sum(m[:, 128 * t : 128 * t + 128] for t in range(tiles))
                q = sum(q[:, 128 * t : 128 * t + 128] for t in range(tiles))
                v = jnp.where(top, m + swap_halves(m), swap_halves(q) - q)
                put(u, jnp.broadcast_to(jnp.sum(v, 1, keepdims=True), (8, 128)))
            return c

        lax.fori_loop(0, users // chunk, body, 0)

    y = forward(lambda u: s_ref[u]) + n_ref[...]
    errs = []
    for layer in range(LAYERS):
        e = y if layer == 0 else y - forward(lambda u: xs_ref[layer, u])
        errs.append(e)
        step = s_ref[users + layer]

        def put(u, v):
            z = step * v if layer == 0 else xs_ref[layer, u] + step * v
            xs_ref[layer + 1, u] = clip_level * jnp.tanh(z * (1.0 / clip_level))

        adjoint(e, put)

    x_out_ref[...] = xs_ref[LAYERS]
    backs = [None] * LAYERS
    for layer in reversed(range(LAYERS)):
        step = s_ref[users + layer]
        last = layer == LAYERS - 1

        def slope(i, c):
            for k in range(chunk):
                u = i * chunk + k
                x = xs_ref[layer + 1, u]
                gx = (x - s_ref[u]) * (2.0 / users) if last else gx_ref[u]
                t = x * (1.0 / clip_level)
                gz_ref[layer, u] = gx * (1.0 - t * t) * step
            return c

        lax.fori_loop(0, users // chunk, slope, 0)
        ge = forward(lambda u: gz_ref[layer, u])
        backs[layer] = ge
        if layer:
            def put(u, v):
                x = xs_ref[layer + 1, u]
                gx = (x - s_ref[u]) * (2.0 / users) if last else gx_ref[u]
                t = x * (1.0 / clip_level)
                gx_ref[u] = gx * (1.0 - t * t) - v

            adjoint(ge, put)

    sign = half_rows((8, ant), 0, 1.0, -1.0)
    pairs = [(v, sign * swap_halves(v)) for k in range(LAYERS) for v in (errs[k], backs[k])]

    def outer(u):
        s = s_ref[u]
        g = jnp.zeros((8, ant), jnp.float32)
        for k in range(LAYERS):
            for which in range(2):
                v, vs = pairs[2 * k + which]
                if which == 0:
                    b = gz_ref[k, u]
                else:
                    b = s - xs_ref[k, u] if k else s
                bs = swap_halves(b)
                g = g + v * wide(jnp.where(top, b, bs)) + vs * wide(jnp.where(top, bs, b))
        g_ref[u] = g

    def body(i, c):
        for k in range(4):
            outer(i * 4 + k)
        return c

    lax.fori_loop(0, users // 4, body, 0)


def detect(channel, symbols, noise):
    users, _, ant = channel.shape
    return pl.pallas_call(
        functools.partial(detect_kernel, users),
        in_specs=[
            pl.BlockSpec(memory_space=pltpu.VMEM),
            pl.BlockSpec(memory_space=pltpu.VMEM),
            pl.BlockSpec(memory_space=pltpu.VMEM),
        ],
        out_specs=[pl.BlockSpec(memory_space=pltpu.VMEM), pl.BlockSpec(memory_space=pltpu.VMEM)],
        out_shape=[
            jax.ShapeDtypeStruct((users, 8, ant), jnp.float32),
            jax.ShapeDtypeStruct((users, 8, 128), jnp.float32),
        ],
        scratch_shapes=[
            pltpu.VMEM((LAYERS + 1, users, 8, 128), jnp.float32),
            pltpu.VMEM((LAYERS, users, 8, 128), jnp.float32),
            pltpu.VMEM((users, 8, 128), jnp.float32),
        ],
        compiler_params=pltpu.CompilerParams(vmem_limit_bytes=16 << 20),
        name="detect",
    )(channel, symbols, noise)


def grad_kernel(n, ul, pw, per, unroll, g_ref, w_ref, e_ref, x_ref, out_ref, lhs_ref, mat_ref):
    u = pl.program_id(0)
    step = pl.program_id(1)
    parts = pw // 128
    ant = g_ref.shape[-1]
    half = ant // 2
    rows = lhs_ref.shape[0]

    @pl.when((u == 0) & (step == 0))
    def _():
        mat_ref[...] = jnp.zeros_like(mat_ref)

    @pl.when(step == 0)
    def _():
        plus = g_ref[:, 0, :, pl.ds(0, half)]
        minus = g_ref[:, 0, :, pl.ds(half, half)]
        odd = swap_halves(plus - minus) * half_rows(plus.shape, 1, -1.0, 1.0)
        mix = jnp.concatenate([plus + minus, odd], 2).reshape(rows, ant)
        high, low = split(mix)
        lhs_ref[:, pl.ds(0, ant)] = high
        lhs_ref[:, pl.ds(ant, ant)] = low

    sign = half_rows((8, pw), 0, 1.0, -1.0)
    kinds = lax.broadcasted_iota(jnp.int32, (MAT, pw), 0).astype(jnp.float32)

    def tile(i, carry):
        s = step * per + i
        w_high = w_ref[0, i, pl.ds(0, ant), :]
        w_low = w_ref[0, i, pl.ds(ant, ant), :]
        l_high = lhs_ref[:, pl.ds(0, ant)]
        left = jnp.concatenate([l_high, lhs_ref[:, pl.ds(ant, ant)]], 0)
        pair = jnp.dot(left, w_high, preferred_element_type=jnp.float32)
        rest = jnp.dot(l_high, w_low, preferred_element_type=jnp.float32)
        q = (pair[:rows] + (pair[rows:] + rest)).reshape(rows // 8, 8, pw)
        e = e_ref[0, i].reshape(rows // 8, 8, pw)
        a = jnp.sum(e * q, 0)
        b = jnp.sum(swap_halves(e) * q, 0)
        p_re = jnp.sum(a * sign, 0, keepdims=True)
        p_im = jnp.sum(b, 0, keepdims=True)
        for t in range(parts):
            lanes = slice(128 * t, 128 * t + 128)
            out_ref[s, pl.ds(t * ul + u, 1), :] = p_re[:, lanes]
            out_ref[s, pl.ds((parts + t) * ul + u, 1), :] = p_im[:, lanes]
        g_re, g_im, mat = (field_row(x_ref, parts, ul, s, j, u) for j in (2, 3, 4))
        along_re = g_re * p_re + g_im * p_im
        along_im = g_re * p_im - g_im * p_re
        hit = jnp.broadcast_to(mat, (MAT, pw)) == kinds
        mat_ref[0] += jnp.where(hit, jnp.broadcast_to(along_re, (MAT, pw)), 0.0)
        mat_ref[1] += jnp.where(hit, jnp.broadcast_to(along_im, (MAT, pw)), 0.0)
        return carry

    lax.fori_loop(0, per, tile, 0, unroll=unroll)

    @pl.when((u == ul - 1) & (step == n // per - 1))
    def _():
        lane = lax.broadcasted_iota(jnp.int32, (MAT, 128), 1)
        kind = lax.broadcasted_iota(jnp.int32, (MAT, 128), 0)
        line = jnp.zeros((1, 128), jnp.float32)
        for j in range(2):
            total = jnp.broadcast_to(jnp.sum(mat_ref[j], 1, keepdims=True), (MAT, 128))
            spread = jnp.where(lane == kind + j * MAT, total, 0.0)
            line = line + jnp.sum(spread, 0, keepdims=True)
        for s in range(n):
            out_ref[s, pl.ds(2 * parts * ul, 1), :] = line


def gradient(grads, steer, tones, params):
    n, ul, _, ant = grads.shape
    wide = params.shape[1]
    pw = steer.shape[-1]
    rows = tones.shape[2]
    sent = 2 * ul * (pw // 128) + 1
    per = n // GRAD_STEPS if n % GRAD_STEPS == 0 else n
    return pl.pallas_call(
        functools.partial(grad_kernel, n, ul, pw, per, min(per, GRAD_UNROLL)),
        grid=(ul, n // per),
        in_specs=[
            pl.BlockSpec((n, 1, 8, ant), lambda u, j: (0, u, 0, 0)),
            pl.BlockSpec((1, per, 2 * ant, pw), lambda u, j: (u, j, 0, 0)),
            pl.BlockSpec((1, per, rows, pw), lambda u, j: (u, j, 0, 0)),
            pl.BlockSpec((n, wide, 128), lambda u, j: (0, 0, 0)),
        ],
        out_specs=pl.BlockSpec((n, sent, 128), lambda u, j: (0, 0, 0)),
        out_shape=jax.ShapeDtypeStruct((n, sent, 128), jnp.float32),
        scratch_shapes=[
            pltpu.VMEM((rows, 2 * ant), jnp.bfloat16),
            pltpu.VMEM((2, MAT, pw), jnp.float32),
        ],
        compiler_params=pltpu.CompilerParams(vmem_limit_bytes=GRAD_VMEM),
        name="gradient",
    )(grads, steer, tones, params)


def exchange(x):
    return lax.all_to_all(x, "path", 0, 0, tiled=True)


def local(
    n,
    path_angle,
    path_delay,
    path_gain,
    material_ids,
    reflection,
    step_sizes,
    tone_ids,
    symbol_ids,
    receiver_noise,
):
    users, pw = path_angle.shape
    own, _, ant = receiver_noise.shape
    assert 2 * own == 8
    half = ant // 2
    ul = users // n
    parts = pw // 128
    params = exchange(pack(n, path_angle, path_delay, path_gain, material_ids))
    tone = tone_ids.astype(jnp.float32) * (1.0 / TONE_SPAN)
    tone = jnp.broadcast_to(tone.reshape(n, 1, own), (n, 2, own)).reshape(8 * n)
    mirror = jnp.broadcast_to(reflection.T[:, :, None], (MAT, 2, 4)).reshape(8 * MAT)
    aux = jnp.concatenate([tone, mirror])
    aux = jnp.broadcast_to(aux[:, None], (8 * (n + MAT), 128))
    channel_rows, steer, tones = synthesize(params, aux, ul, pw, ant)
    channel = exchange(channel_rows).reshape(users, 8, ant)

    symbols = jnp.stack([symbol_ids % 4, symbol_ids // 4], 0)
    symbols = (2 * symbols - 3).astype(jnp.float32) * qam_scale
    symbols = jnp.transpose(symbols, (2, 0, 1)).reshape(users, 8)
    symbols = jnp.concatenate([symbols, jnp.broadcast_to(step_sizes[:, None], (LAYERS, 8))], 0)
    symbols = jnp.broadcast_to(symbols[:, :, None], (users + LAYERS, 8, 128))
    noise = jnp.transpose(receiver_noise, (1, 0, 2)).reshape(8, ant)
    noise = jnp.concatenate([noise[:, half:], noise[:, :half][:, ::-1]], 1)
    grads, found = detect(channel, symbols, noise)
    estimates = jnp.transpose(found[:, :, 0].reshape(users, 2, own), (2, 1, 0))

    grads = exchange(grads.reshape(n, ul, 8, ant))
    sent = gradient(grads, steer, tones, params)
    back = exchange(sent)
    wide = 2 * parts * ul
    path_grad = jnp.transpose(back[:, :wide].reshape(n, 2, parts, ul, 128), (1, 0, 3, 2, 4))
    path_grad = path_grad.reshape(2, users, pw)
    material_grad = jnp.sum(back[:, wide, : 2 * MAT], 0).reshape(2, MAT)

    responses = jnp.transpose(channel.reshape(users, 2, own, ant), (2, 1, 0, 3))
    responses = jnp.concatenate([responses[..., half:][..., ::-1], responses[..., :half]], -1)
    return (path_grad, estimates, material_grad, responses)


def solution(mesh):
    in_specs = (
        P(None, ("groups", "path")),
        P(None, ("groups", "path")),
        P(None, None, ("groups", "path")),
        P(None, ("groups", "path")),
        P(),
        P(),
        P("groups"),
        P(("groups", "path"), None),
        P(("groups", "path"), None, None),
    )
    out_specs = (
        P(None, None, ("groups", "path")),
        P(("groups", "path"), None, None),
        P(None, "groups"),
        P(("groups", "path"), None, None, None),
    )
    body = functools.partial(local, mesh.shape["path"])
    return jax.shard_map(body, mesh=mesh, in_specs=in_specs, out_specs=out_specs, check_vma=False)
```

```python
import functools
import math

import jax
import jax.numpy as jnp
import numpy as np
from jax import lax
from jax.experimental import pallas as pl
from jax.experimental.pallas import tpu as pltpu
from jax.sharding import PartitionSpec as P

MAT = 16
TONE_SPAN = 3276
LAYERS = 4
FIELDS = 5

SYNTH_VMEM = 48 << 20
GRAD_VMEM = 48 << 20
SYNTH_UNROLL = 4
GRAD_UNROLL = 8
DETECT_UNROLL = 64
GRAD_STEPS = 1

clip_level = 1.5
qam_scale = 1.0 / math.sqrt(10.0)

SINE = (
    6.283185160088971,
    -41.341655031286386,
    81.60100406453228,
    -76.5497820808334,
    39.536704364112744,
)


def cos_turns(t):
    a = 0.25 - jnp.abs(t - jnp.round(t))
    z = a * a
    p = SINE[4] * z + SINE[3]
    p = p * z + SINE[2]
    p = p * z + SINE[1]
    p = p * z + SINE[0]
    return p * a


RISE = (
    -0.16666660462354993,
    0.00833308816681783,
    -0.00019811112712181806,
    2.6089325665533767e-06,
)


def sine(angle):
    t = jnp.abs(angle)
    y = jnp.where(t > 0.5 * math.pi, (3.140625 - t) + (math.pi - 3.140625), t)
    z = y * y
    p = RISE[3] * z + RISE[2]
    p = p * z + RISE[1]
    p = p * z + RISE[0]
    s = y + (y * z) * p
    return jnp.where(angle < 0.0, -s, s)


def swap_halves(x):
    return pltpu.roll(x, 4, x.ndim - 2)


def half_rows(shape, dim, top, bottom):
    row = lax.broadcasted_iota(jnp.int32, shape, dim)
    return jnp.where(row % 8 < 4, jnp.float32(top), jnp.float32(bottom))


def top_mask(shape, dim):
    return lax.broadcasted_iota(jnp.int32, shape, dim) % 8 < 4


def split(x):
    high = x.astype(jnp.bfloat16)
    low = (x - high.astype(jnp.float32)).astype(jnp.bfloat16)
    return high, low


def pack_kernel(n, ul, angle_ref, delay_ref, gain_ref, ids_ref, out_ref):
    pw = angle_ref.shape[-1]
    fields = (
        0.5 * sine(angle_ref[...]),
        delay_ref[...],
        gain_ref[0],
        gain_ref[1],
        ids_ref[...].astype(jnp.float32),
    )
    parts = pw // 128
    for j, field in enumerate(fields):
        for t in range(parts):
            block = field[:, 128 * t : 128 * t + 128]
            for d in range(n):
                start = (j * parts + t) * ul
                out_ref[d, pl.ds(start, ul), :] = block[d * ul : d * ul + ul]


def pack(n, angle, delay, gain, ids):
    users, pw = angle.shape
    ul = users // n
    rows = FIELDS * ul * (pw // 128)
    return pl.pallas_call(
        functools.partial(pack_kernel, n, ul),
        in_specs=[pl.BlockSpec(memory_space=pltpu.VMEM)] * 4,
        out_specs=pl.BlockSpec(memory_space=pltpu.VMEM),
        out_shape=jax.ShapeDtypeStruct((n, rows, 128), jnp.float32),
        compiler_params=pltpu.CompilerParams(vmem_limit_bytes=60 << 20),
        name="pack",
    )(angle, delay, gain, ids)


def field_row(x_ref, parts, ul, s, j, u):
    rows = [x_ref[s, pl.ds((j * parts + t) * ul + u, 1), :] for t in range(parts)]
    return jnp.concatenate(rows, 1)


def synth_kernel(n, ul, pw, unroll, x_ref, aux_ref, h_ref, w_ref, e_ref, lhs_ref, acc_ref):
    u = pl.program_id(0)
    parts = pw // 128
    half = w_ref.shape[-2] // 4
    rows = acc_ref.shape[0]
    top8 = top_mask((8, pw), 0)
    shift8 = half_rows((8, pw), 0, 0.0, -0.25)
    blocks = half // 16
    fine_row = lax.broadcasted_iota(jnp.int32, (16, pw), 0)
    fine_coef = (fine_row % 8).astype(jnp.float32) + 0.5
    fine_shift = jnp.where(fine_row < 8, 0.0, -0.25)
    coarse_row = lax.broadcasted_iota(jnp.int32, (2 * blocks, pw), 0)
    coarse_coef = (coarse_row % blocks).astype(jnp.float32) * 16.0 + 8.0
    coarse_shift = jnp.where(coarse_row < blocks, 0.0, -0.25)

    def wide(m):
        block = aux_ref[pl.ds(rows + 8 * m, 8), :]
        return jnp.concatenate([block] * parts, 1)

    def tile(s, carry):
        w, dly, g_re, g_im, mat = (field_row(x_ref, parts, ul, s, j, u) for j in range(FIELDS))
        w8 = jnp.broadcast_to(w, (8, pw))
        fine = cos_turns(fine_coef * jnp.concatenate([w8] * 2, 0) + fine_shift)
        w16 = jnp.concatenate([w8] * (2 * blocks // 8), 0)
        coarse = cos_turns(coarse_coef * w16 + coarse_shift)
        f_cos, f_sin = fine[:8], fine[8:]
        for b in range(blocks):
            c_cos = coarse[b : b + 1]
            c_sin = coarse[blocks + b : blocks + b + 1]
            cc, ss = c_cos * f_cos, c_sin * f_sin
            sc, cs = c_sin * f_cos, c_cos * f_sin
            a_cos = jnp.concatenate([cc - ss, cc + ss], 0)
            a_sin = jnp.concatenate([sc + cs, sc - cs], 0)
            for base, val in ((0, a_cos), (half, a_sin)):
                high, low = split(val)
                w_ref[0, s, pl.ds(base + 16 * b, 16), :] = high
                w_ref[0, s, pl.ds(2 * half + base + 16 * b, 16), :] = low
        mat8 = jnp.broadcast_to(mat, (8, pw)).astype(jnp.int32)
        level = [wide(m) for m in range(MAT)]
        for bit in range(MAT.bit_length() - 1):
            hit = (mat8 & (1 << bit)) != 0
            level = [jnp.where(hit, y, x) for x, y in zip(level[::2], level[1::2])]
        refl = level[0]
        flip = swap_halves(refl)
        r_re, r_im = jnp.where(top8, refl, flip), jnp.where(top8, flip, refl)
        c_re = g_re * r_re - g_im * r_im
        c_im = g_re * r_im + g_im * r_re
        c_mix = jnp.where(top8, c_re, -c_re)
        centre = w * (half - 0.5)
        centre = centre - jnp.round(centre)
        base8 = shift8 + centre
        d8 = jnp.broadcast_to(dly, (8, pw))
        step = 32
        for q in range(rows // step):
            rq = pl.ds(q * step, step)
            tone = aux_ref[rq, :]
            tone = jnp.concatenate([tone] * parts, 1)
            d32 = jnp.concatenate([d8] * (step // 8), 0)
            b32 = jnp.concatenate([base8] * (step // 8), 0)
            e = cos_turns(tone * d32 + b32)
            e_ref[0, s, rq, :] = e
            e3 = e.reshape(step // 8, 8, pw)
            g = e3 * c_mix[None] + swap_halves(e3) * c_im[None]
            high, low = split(g.reshape(step, pw))
            lhs_ref[s % 2, rq, pl.ds(0, pw)] = high
            lhs_ref[s % 2, rq, pl.ds(pw, pw)] = low
        dims = (((1,), (1,)), ((), ()))
        w_high = w_ref[0, s, pl.ds(0, 2 * half), :]
        w_low = w_ref[0, s, pl.ds(2 * half, 2 * half), :]
        l_high = lhs_ref[s % 2, :, pl.ds(0, pw)]
        left = jnp.concatenate([l_high, lhs_ref[s % 2, :, pl.ds(pw, pw)]], 0)
        pair = lax.dot_general(left, w_high, dims, preferred_element_type=jnp.float32)
        rest = lax.dot_general(l_high, w_low, dims, preferred_element_type=jnp.float32)
        acc_ref[...] += pair[:rows] + (pair[rows:] + rest)
        return carry

    acc_ref[...] = jnp.zeros_like(acc_ref)
    lax.fori_loop(0, n, tile, 0, unroll=unroll)
    even = acc_ref[:, pl.ds(0, half)].reshape(rows // 8, 8, half)
    odd = acc_ref[:, pl.ds(half, half)].reshape(rows // 8, 8, half)
    odd = swap_halves(odd) * half_rows(odd.shape, 1, 1.0, -1.0)
    h_ref[:, 0, :, pl.ds(0, half)] = even + odd
    h_ref[:, 0, :, pl.ds(half, half)] = even - odd


def synthesize(params, aux, ul, pw, antennas):
    n, wide, _ = params.shape
    rows = 8 * n
    return pl.pallas_call(
        functools.partial(synth_kernel, n, ul, pw, min(n, SYNTH_UNROLL)),
        grid=(ul,),
        in_specs=[
            pl.BlockSpec((n, wide, 128), lambda u: (0, 0, 0)),
            pl.BlockSpec(aux.shape, lambda u: (0, 0)),
        ],
        out_specs=[
            pl.BlockSpec((n, 1, 8, antennas), lambda u: (0, u, 0, 0)),
            pl.BlockSpec((1, n, 2 * antennas, pw), lambda u: (u, 0, 0, 0)),
            pl.BlockSpec((1, n, rows, pw), lambda u: (u, 0, 0, 0)),
        ],
        out_shape=[
            jax.ShapeDtypeStruct((n, ul, 8, antennas), jnp.float32),
            jax.ShapeDtypeStruct((ul, n, 2 * antennas, pw), jnp.bfloat16),
            jax.ShapeDtypeStruct((ul, n, rows, pw), jnp.float32),
        ],
        scratch_shapes=[
            pltpu.VMEM((2, rows, 2 * pw), jnp.bfloat16),
            pltpu.VMEM((rows, antennas), jnp.float32),
        ],
        compiler_params=pltpu.CompilerParams(vmem_limit_bytes=SYNTH_VMEM),
        name="synth",
    )(params, aux)


def detect_kernel(users, h_ref, s_ref, n_ref, g_ref, x_out_ref, xs_ref, gz_ref, gx_ref):
    ant = h_ref.shape[-1]
    tiles = ant // 128
    top = top_mask((8, 128), 0)
    top_a = top_mask((8, ant), 0)
    chunk = DETECT_UNROLL

    def wide(x):
        return jnp.concatenate([x] * tiles, 1) if tiles > 1 else x

    def forward(get):
        def body(i, c):
            c = list(c)
            for k in range(chunk):
                u = i * chunk + k
                h = h_ref[u]
                x = get(u)
                j = 2 * (k % 4)
                c[j] = c[j] + h * wide(x)
                c[j + 1] = c[j + 1] + h * wide(swap_halves(x))
            return tuple(c)

        zero = jnp.zeros((8, ant), jnp.float32)
        c = lax.fori_loop(0, users // chunk, body, (zero,) * 8)
        a = (c[0] + c[2]) + (c[4] + c[6])
        b = (c[1] + c[3]) + (c[5] + c[7])
        return jnp.where(top_a, a - swap_halves(a), b + swap_halves(b))

    def adjoint(e, put):
        es = swap_halves(e)

        def body(i, c):
            for k in range(chunk):
                u = i * chunk + k
                h = h_ref[u]
                m, q = h * e, h * es
                m = sum(m[:, 128 * t : 128 * t + 128] for t in range(tiles))
                q = sum(q[:, 128 * t : 128 * t + 128] for t in range(tiles))
                v = jnp.where(top, m + swap_halves(m), swap_halves(q) - q)
                put(u, jnp.broadcast_to(jnp.sum(v, 1, keepdims=True), (8, 128)))
            return c

        lax.fori_loop(0, users // chunk, body, 0)

    y = forward(lambda u: s_ref[u]) + n_ref[...]
    errs = []
    for layer in range(LAYERS):
        e = y if layer == 0 else y - forward(lambda u: xs_ref[layer, u])
        errs.append(e)
        step = s_ref[users + layer]

        def put(u, v):
            z = step * v if layer == 0 else xs_ref[layer, u] + step * v
            xs_ref[layer + 1, u] = clip_level * jnp.tanh(z * (1.0 / clip_level))

        adjoint(e, put)

    x_out_ref[...] = xs_ref[LAYERS]
    backs = [None] * LAYERS
    for layer in reversed(range(LAYERS)):
        step = s_ref[users + layer]
        last = layer == LAYERS - 1

        def slope(i, c):
            for k in range(chunk):
                u = i * chunk + k
                x = xs_ref[layer + 1, u]
                gx = (x - s_ref[u]) * (2.0 / users) if last else gx_ref[u]
                t = x * (1.0 / clip_level)
                gz_ref[layer, u] = gx * (1.0 - t * t) * step
            return c

        lax.fori_loop(0, users // chunk, slope, 0)
        ge = forward(lambda u: gz_ref[layer, u])
        backs[layer] = ge
        if layer:
            def put(u, v):
                x = xs_ref[layer + 1, u]
                gx = (x - s_ref[u]) * (2.0 / users) if last else gx_ref[u]
                t = x * (1.0 / clip_level)
                gx_ref[u] = gx * (1.0 - t * t) - v

            adjoint(ge, put)

    sign = half_rows((8, ant), 0, 1.0, -1.0)
    pairs = [(v, sign * swap_halves(v)) for k in range(LAYERS) for v in (errs[k], backs[k])]

    def outer(u):
        s = s_ref[u]
        g = jnp.zeros((8, ant), jnp.float32)
        for k in range(LAYERS):
            for which in range(2):
                v, vs = pairs[2 * k + which]
                if which == 0:
                    b = gz_ref[k, u]
                else:
                    b = s - xs_ref[k, u] if k else s
                bs = swap_halves(b)
                g = g + v * wide(jnp.where(top, b, bs)) + vs * wide(jnp.where(top, bs, b))
        g_ref[u] = g

    def body(i, c):
        for k in range(4):
            outer(i * 4 + k)
        return c

    lax.fori_loop(0, users // 4, body, 0)


def detect(channel, symbols, noise):
    users, _, ant = channel.shape
    return pl.pallas_call(
        functools.partial(detect_kernel, users),
        in_specs=[
            pl.BlockSpec(memory_space=pltpu.VMEM),
            pl.BlockSpec(memory_space=pltpu.VMEM),
            pl.BlockSpec(memory_space=pltpu.VMEM),
        ],
        out_specs=[pl.BlockSpec(memory_space=pltpu.VMEM), pl.BlockSpec(memory_space=pltpu.VMEM)],
        out_shape=[
            jax.ShapeDtypeStruct((users, 8, ant), jnp.float32),
            jax.ShapeDtypeStruct((users, 8, 128), jnp.float32),
        ],
        scratch_shapes=[
            pltpu.VMEM((LAYERS + 1, users, 8, 128), jnp.float32),
            pltpu.VMEM((LAYERS, users, 8, 128), jnp.float32),
            pltpu.VMEM((users, 8, 128), jnp.float32),
        ],
        compiler_params=pltpu.CompilerParams(vmem_limit_bytes=16 << 20),
        name="detect",
    )(channel, symbols, noise)


def grad_kernel(n, ul, pw, per, unroll, g_ref, w_ref, e_ref, x_ref, out_ref, lhs_ref, mat_ref):
    u = pl.program_id(0)
    step = pl.program_id(1)
    parts = pw // 128
    ant = g_ref.shape[-1]
    half = ant // 2
    rows = lhs_ref.shape[0]

    @pl.when((u == 0) & (step == 0))
    def _():
        mat_ref[...] = jnp.zeros_like(mat_ref)

    @pl.when(step == 0)
    def _():
        plus = g_ref[:, 0, :, pl.ds(0, half)]
        minus = g_ref[:, 0, :, pl.ds(half, half)]
        odd = swap_halves(plus - minus) * half_rows(plus.shape, 1, -1.0, 1.0)
        mix = jnp.concatenate([plus + minus, odd], 2).reshape(rows, ant)
        high, low = split(mix)
        lhs_ref[:, pl.ds(0, ant)] = high
        lhs_ref[:, pl.ds(ant, ant)] = low

    sign = half_rows((8, pw), 0, 1.0, -1.0)
    kinds = lax.broadcasted_iota(jnp.int32, (MAT, pw), 0).astype(jnp.float32)

    def tile(i, carry):
        s = step * per + i
        w_high = w_ref[0, i, pl.ds(0, ant), :]
        w_low = w_ref[0, i, pl.ds(ant, ant), :]
        l_high = lhs_ref[:, pl.ds(0, ant)]
        left = jnp.concatenate([l_high, lhs_ref[:, pl.ds(ant, ant)]], 0)
        pair = jnp.dot(left, w_high, preferred_element_type=jnp.float32)
        rest = jnp.dot(l_high, w_low, preferred_element_type=jnp.float32)
        q = (pair[:rows] + (pair[rows:] + rest)).reshape(rows // 8, 8, pw)
        e = e_ref[0, i].reshape(rows // 8, 8, pw)
        a = jnp.sum(e * q, 0)
        b = jnp.sum(swap_halves(e) * q, 0)
        p_re = jnp.sum(a * sign, 0, keepdims=True)
        p_im = jnp.sum(b, 0, keepdims=True)
        for t in range(parts):
            lanes = slice(128 * t, 128 * t + 128)
            out_ref[s, pl.ds(t * ul + u, 1), :] = p_re[:, lanes]
            out_ref[s, pl.ds((parts + t) * ul + u, 1), :] = p_im[:, lanes]
        g_re, g_im, mat = (field_row(x_ref, parts, ul, s, j, u) for j in (2, 3, 4))
        along_re = g_re * p_re + g_im * p_im
        along_im = g_re * p_im - g_im * p_re
        hit = jnp.broadcast_to(mat, (MAT, pw)) == kinds
        mat_ref[0] += jnp.where(hit, jnp.broadcast_to(along_re, (MAT, pw)), 0.0)
        mat_ref[1] += jnp.where(hit, jnp.broadcast_to(along_im, (MAT, pw)), 0.0)
        return carry

    lax.fori_loop(0, per, tile, 0, unroll=unroll)

    @pl.when((u == ul - 1) & (step == n // per - 1))
    def _():
        lane = lax.broadcasted_iota(jnp.int32, (MAT, 128), 1)
        kind = lax.broadcasted_iota(jnp.int32, (MAT, 128), 0)
        line = jnp.zeros((1, 128), jnp.float32)
        for j in range(2):
            total = jnp.broadcast_to(jnp.sum(mat_ref[j], 1, keepdims=True), (MAT, 128))
            spread = jnp.where(lane == kind + j * MAT, total, 0.0)
            line = line + jnp.sum(spread, 0, keepdims=True)
        for s in range(n):
            out_ref[s, pl.ds(2 * parts * ul, 1), :] = line


def gradient(grads, steer, tones, params):
    n, ul, _, ant = grads.shape
    wide = params.shape[1]
    pw = steer.shape[-1]
    rows = tones.shape[2]
    sent = 2 * ul * (pw // 128) + 1
    per = n // GRAD_STEPS if n % GRAD_STEPS == 0 else n
    return pl.pallas_call(
        functools.partial(grad_kernel, n, ul, pw, per, min(per, GRAD_UNROLL)),
        grid=(ul, n // per),
        in_specs=[
            pl.BlockSpec((n, 1, 8, ant), lambda u, j: (0, u, 0, 0)),
            pl.BlockSpec((1, per, 2 * ant, pw), lambda u, j: (u, j, 0, 0)),
            pl.BlockSpec((1, per, rows, pw), lambda u, j: (u, j, 0, 0)),
            pl.BlockSpec((n, wide, 128), lambda u, j: (0, 0, 0)),
        ],
        out_specs=pl.BlockSpec((n, sent, 128), lambda u, j: (0, 0, 0)),
        out_shape=jax.ShapeDtypeStruct((n, sent, 128), jnp.float32),
        scratch_shapes=[
            pltpu.VMEM((rows, 2 * ant), jnp.bfloat16),
            pltpu.VMEM((2, MAT, pw), jnp.float32),
        ],
        compiler_params=pltpu.CompilerParams(vmem_limit_bytes=GRAD_VMEM),
        name="gradient",
    )(grads, steer, tones, params)


def unpack_kernel(n, ul, x_ref, grad_ref, mat_ref):
    parts = grad_ref.shape[-1] // 128
    total = x_ref[0, pl.ds(2 * parts * ul, 1), :]
    for s in range(1, n):
        total = total + x_ref[s, pl.ds(2 * parts * ul, 1), :]
    for j in range(2):
        mat_ref[pl.ds(j, 1), :] = total[:, j * MAT : j * MAT + MAT]
    for s in range(n):
        for j in range(2):
            for t in range(parts):
                rows = x_ref[s, pl.ds((j * parts + t) * ul, ul), :]
                grad_ref[j, pl.ds(s * ul, ul), pl.ds(128 * t, 128)] = rows


def unpack(received, users, pw):
    n = received.shape[0]
    return pl.pallas_call(
        functools.partial(unpack_kernel, n, users // n),
        in_specs=[pl.BlockSpec(memory_space=pltpu.VMEM)],
        out_specs=[pl.BlockSpec(memory_space=pltpu.VMEM)] * 2,
        out_shape=[
            jax.ShapeDtypeStruct((2, users, pw), jnp.float32),
            jax.ShapeDtypeStruct((2, MAT), jnp.float32),
        ],
        compiler_params=pltpu.CompilerParams(vmem_limit_bytes=8 << 20),
        name="unpack",
    )(received)


def antenna_order(ant):
    half = ant // 2
    offset = np.arange(half).reshape(-1, 2, 8)
    offset = np.stack([offset[:, 1], offset[:, 0, ::-1]], 1).reshape(half)
    return np.concatenate([half + offset, half - 1 - offset])


def exchange(x):
    return lax.all_to_all(x, "path", 0, 0, tiled=True)


def local(
    n,
    path_angle,
    path_delay,
    path_gain,
    material_ids,
    reflection,
    step_sizes,
    tone_ids,
    symbol_ids,
    receiver_noise,
):
    users, pw = path_angle.shape
    own, _, ant = receiver_noise.shape
    assert 2 * own == 8
    ul = users // n
    params = exchange(pack(n, path_angle, path_delay, path_gain, material_ids))
    tone = tone_ids.astype(jnp.float32) * (1.0 / TONE_SPAN)
    tone = jnp.broadcast_to(tone.reshape(n, 1, own), (n, 2, own)).reshape(8 * n)
    mirror = jnp.broadcast_to(reflection.T[:, :, None], (MAT, 2, 4)).reshape(8 * MAT)
    aux = jnp.concatenate([tone, mirror])
    aux = jnp.broadcast_to(aux[:, None], (8 * (n + MAT), 128))
    channel_rows, steer, tones = synthesize(params, aux, ul, pw, ant)
    channel = exchange(channel_rows).reshape(users, 8, ant)

    symbols = jnp.stack([symbol_ids % 4, symbol_ids // 4], 0)
    symbols = (2 * symbols - 3).astype(jnp.float32) * qam_scale
    symbols = jnp.transpose(symbols, (2, 0, 1)).reshape(users, 8)
    symbols = jnp.concatenate([symbols, jnp.broadcast_to(step_sizes[:, None], (LAYERS, 8))], 0)
    symbols = jnp.broadcast_to(symbols[:, :, None], (users + LAYERS, 8, 128))
    noise = jnp.transpose(receiver_noise, (1, 0, 2)).reshape(8, ant)
    order = jnp.asarray(antenna_order(ant), jnp.int32)
    place = (order[None] == jnp.arange(ant, dtype=jnp.int32)[:, None]).astype(jnp.float32)
    noise = jnp.dot(noise, place, precision=lax.Precision.HIGHEST)
    grads, found = detect(channel, symbols, noise)
    estimates = jnp.transpose(found[:, :, 0].reshape(users, 2, own), (2, 1, 0))

    grads = exchange(grads.reshape(n, ul, 8, ant))
    sent = gradient(grads, steer, tones, params)
    back = exchange(sent)
    path_grad, material_grad = unpack(back, users, pw)

    responses = jnp.transpose(channel.reshape(users, 2, own, ant), (2, 1, 0, 3))
    responses = jnp.einsum("...k,ak->...a", responses, place, precision=lax.Precision.HIGHEST)
    return (path_grad, estimates, material_grad, responses)


def solution(mesh):
    in_specs = (
        P(None, ("groups", "path")),
        P(None, ("groups", "path")),
        P(None, None, ("groups", "path")),
        P(None, ("groups", "path")),
        P(),
        P(),
        P("groups"),
        P(("groups", "path"), None),
        P(("groups", "path"), None, None),
    )
    out_specs = (
        P(None, None, ("groups", "path")),
        P(("groups", "path"), None, None),
        P(None, "groups"),
        P(("groups", "path"), None, None, None),
    )
    body = functools.partial(local, mesh.shape["path"])
    return jax.shard_map(body, mesh=mesh, in_specs=in_specs, out_specs=out_specs, check_vma=False)
```

```python
import functools
import math

import jax
import jax.numpy as jnp
import numpy as np
from jax import lax
from jax.experimental import pallas as pl
from jax.experimental.pallas import tpu as pltpu
from jax.sharding import PartitionSpec as P

MAT = 16
TONE_SPAN = 3276
LAYERS = 4
FIELDS = 5

SYNTH_VMEM = 48 << 20
GRAD_VMEM = 48 << 20
SYNTH_UNROLL = 16
SYNTH_JOINED = 16
GRAD_UNROLL = 16
DETECT_UNROLL = 64
GRAD_STEPS = 1

clip_level = 1.5
qam_scale = 1.0 / math.sqrt(10.0)

SINE = (
    6.283185160088971,
    -41.341655031286386,
    81.60100406453228,
    -76.5497820808334,
    39.536704364112744,
)


def cos_turns(t):
    a = 0.25 - jnp.abs(t - jnp.round(t))
    z = a * a
    p = SINE[4] * z + SINE[3]
    p = p * z + SINE[2]
    p = p * z + SINE[1]
    p = p * z + SINE[0]
    return p * a


RISE = (
    -0.16666660462354993,
    0.00833308816681783,
    -0.00019811112712181806,
    2.6089325665533767e-06,
)


def sine(angle):
    t = jnp.abs(angle)
    y = jnp.where(t > 0.5 * math.pi, (3.140625 - t) + (math.pi - 3.140625), t)
    z = y * y
    p = RISE[3] * z + RISE[2]
    p = p * z + RISE[1]
    p = p * z + RISE[0]
    s = y + (y * z) * p
    return jnp.where(angle < 0.0, -s, s)


def swap_halves(x):
    return pltpu.roll(x, 4, x.ndim - 2)


def half_rows(shape, dim, top, bottom):
    row = lax.broadcasted_iota(jnp.int32, shape, dim)
    return jnp.where(row % 8 < 4, jnp.float32(top), jnp.float32(bottom))


def top_mask(shape, dim):
    return lax.broadcasted_iota(jnp.int32, shape, dim) % 8 < 4


def split(x):
    high = x.astype(jnp.bfloat16)
    low = (x - high.astype(jnp.float32)).astype(jnp.bfloat16)
    return high, low


def pack_kernel(n, ul, angle_ref, delay_ref, gain_ref, ids_ref, out_ref):
    pw = angle_ref.shape[-1]
    fields = (
        0.5 * sine(angle_ref[...]),
        delay_ref[...],
        gain_ref[0],
        gain_ref[1],
        ids_ref[...].astype(jnp.float32),
    )
    parts = pw // 128
    for j, field in enumerate(fields):
        for t in range(parts):
            block = field[:, 128 * t : 128 * t + 128]
            for d in range(n):
                start = (j * parts + t) * ul
                out_ref[d, pl.ds(start, ul), :] = block[d * ul : d * ul + ul]


def pack(n, angle, delay, gain, ids):
    users, pw = angle.shape
    ul = users // n
    rows = FIELDS * ul * (pw // 128)
    return pl.pallas_call(
        functools.partial(pack_kernel, n, ul),
        in_specs=[pl.BlockSpec(memory_space=pltpu.VMEM)] * 4,
        out_specs=pl.BlockSpec(memory_space=pltpu.VMEM),
        out_shape=jax.ShapeDtypeStruct((n, rows, 128), jnp.float32),
        compiler_params=pltpu.CompilerParams(vmem_limit_bytes=60 << 20),
        name="pack",
    )(angle, delay, gain, ids)


def field_row(x_ref, parts, ul, s, j, u):
    rows = [x_ref[s, pl.ds((j * parts + t) * ul + u, 1), :] for t in range(parts)]
    return jnp.concatenate(rows, 1)


def steering(fine, coarse, w_ref, slot):
    blocks = coarse.shape[0] // 2
    half = 16 * blocks
    f_cos, f_sin = fine[:8], fine[8:]
    for b in range(blocks):
        c_cos = coarse[b : b + 1]
        c_sin = coarse[blocks + b : blocks + b + 1]
        cc, ss = c_cos * f_cos, c_sin * f_sin
        sc, cs = c_sin * f_cos, c_cos * f_sin
        a_cos = jnp.concatenate([cc - ss, cc + ss], 0)
        a_sin = jnp.concatenate([sc + cs, sc - cs], 0)
        for base, val in ((0, a_cos), (half, a_sin)):
            high, low = split(val)
            w_ref[slot, pl.ds(base + 16 * b, 16), :] = high
            w_ref[slot, pl.ds(2 * half + base + 16 * b, 16), :] = low


def synth_kernel(n, ul, pw, unroll, x_ref, aux_ref, h_ref, e_ref, w_ref, lhs_ref, acc_ref):
    u = pl.program_id(0)
    parts = pw // 128
    half = acc_ref.shape[-1] // 2
    rows = acc_ref.shape[0]
    top8 = top_mask((8, pw), 0)
    shift8 = half_rows((8, pw), 0, 0.0, -0.25)
    blocks = half // 16
    fine_row = lax.broadcasted_iota(jnp.int32, (16, pw), 0)
    fine_coef = (fine_row % 8).astype(jnp.float32) + 0.5
    fine_shift = jnp.where(fine_row < 8, 0.0, -0.25)
    coarse_row = lax.broadcasted_iota(jnp.int32, (2 * blocks, pw), 0)
    coarse_coef = (coarse_row % blocks).astype(jnp.float32) * 16.0 + 8.0
    coarse_shift = jnp.where(coarse_row < blocks, 0.0, -0.25)

    def wide(m):
        block = aux_ref[pl.ds(rows + 8 * m, 8), :]
        return jnp.concatenate([block] * parts, 1)

    def tile(s, slot):
        w, dly, g_re, g_im, mat = (field_row(x_ref, parts, ul, s, j, u) for j in range(FIELDS))
        w8 = jnp.broadcast_to(w, (8, pw))
        fine = cos_turns(fine_coef * jnp.concatenate([w8] * 2, 0) + fine_shift)
        w16 = jnp.concatenate([w8] * (2 * blocks // 8), 0)
        coarse = cos_turns(coarse_coef * w16 + coarse_shift)
        e_ref[0, s, pl.ds(rows, 16), :] = fine
        e_ref[0, s, pl.ds(rows + 16, 2 * blocks), :] = coarse
        steering(fine, coarse, w_ref, slot)
        mat8 = jnp.broadcast_to(mat, (8, pw)).astype(jnp.int32)
        level = [wide(m) for m in range(MAT)]
        for bit in range(MAT.bit_length() - 1):
            hit = (mat8 & (1 << bit)) != 0
            level = [jnp.where(hit, y, x) for x, y in zip(level[::2], level[1::2])]
        refl = level[0]
        flip = swap_halves(refl)
        r_re, r_im = jnp.where(top8, refl, flip), jnp.where(top8, flip, refl)
        c_re = g_re * r_re - g_im * r_im
        c_im = g_re * r_im + g_im * r_re
        c_mix = jnp.where(top8, c_re, -c_re)
        centre = w * (half - 0.5)
        centre = centre - jnp.round(centre)
        base8 = shift8 + centre
        d8 = jnp.broadcast_to(dly, (8, pw))
        step = 32
        for q in range(rows // step):
            rq = pl.ds(q * step, step)
            tone = aux_ref[rq, :]
            tone = jnp.concatenate([tone] * parts, 1)
            d32 = jnp.concatenate([d8] * (step // 8), 0)
            b32 = jnp.concatenate([base8] * (step // 8), 0)
            e = cos_turns(tone * d32 + b32)
            e_ref[0, s, rq, :] = e
            e3 = e.reshape(step // 8, 8, pw)
            g = e3 * c_mix[None] + swap_halves(e3) * c_im[None]
            high, low = split(g.reshape(step, pw))
            lhs_ref[slot, rq, pl.ds(0, pw)] = high
            lhs_ref[slot, rq, pl.ds(pw, pw)] = low

    def product(slots):
        def lhs(base):
            return jnp.concatenate([lhs_ref[k, :, pl.ds(base, pw)] for k in slots], 1)

        def steer(base):
            return jnp.concatenate([w_ref[k, pl.ds(base, 2 * half), :] for k in slots], 1)

        dims = (((1,), (1,)), ((), ()))
        l_high = lhs(0)
        left = jnp.concatenate([l_high, lhs(pw)], 0)
        pair = lax.dot_general(left, steer(0), dims, preferred_element_type=jnp.float32)
        rest = lax.dot_general(l_high, steer(2 * half), dims, preferred_element_type=jnp.float32)
        acc_ref[...] += pair[:rows] + (pair[rows:] + rest)

    joined = math.gcd(unroll, SYNTH_JOINED)

    def group(i, carry):
        for first in range(0, unroll, joined):
            slots = range(first, first + joined)
            for slot in slots:
                tile(i * unroll + slot, slot)
            product(slots)
        return carry

    acc_ref[...] = jnp.zeros_like(acc_ref)
    lax.fori_loop(0, n // unroll, group, 0)
    even = acc_ref[:, pl.ds(0, half)].reshape(rows // 8, 8, half)
    odd = acc_ref[:, pl.ds(half, half)].reshape(rows // 8, 8, half)
    odd = swap_halves(odd) * half_rows(odd.shape, 1, 1.0, -1.0)
    h_ref[:, 0, :, pl.ds(0, half)] = even + odd
    h_ref[:, 0, :, pl.ds(half, half)] = even - odd


def synthesize(params, aux, ul, pw, antennas):
    n, wide, _ = params.shape
    rows = 8 * n
    kept = rows + 16 + antennas // 16
    unroll = math.gcd(n, SYNTH_UNROLL)
    return pl.pallas_call(
        functools.partial(synth_kernel, n, ul, pw, unroll),
        grid=(ul,),
        in_specs=[
            pl.BlockSpec((n, wide, 128), lambda u: (0, 0, 0)),
            pl.BlockSpec(aux.shape, lambda u: (0, 0)),
        ],
        out_specs=[
            pl.BlockSpec((n, 1, 8, antennas), lambda u: (0, u, 0, 0)),
            pl.BlockSpec((1, n, kept, pw), lambda u: (u, 0, 0, 0)),
        ],
        out_shape=[
            jax.ShapeDtypeStruct((n, ul, 8, antennas), jnp.float32),
            jax.ShapeDtypeStruct((ul, n, kept, pw), jnp.float32),
        ],
        scratch_shapes=[
            pltpu.VMEM((unroll, 2 * antennas, pw), jnp.bfloat16),
            pltpu.VMEM((unroll, rows, 2 * pw), jnp.bfloat16),
            pltpu.VMEM((rows, antennas), jnp.float32),
        ],
        compiler_params=pltpu.CompilerParams(vmem_limit_bytes=SYNTH_VMEM),
        name="synth",
    )(params, aux)


def detect_kernel(users, h_ref, s_ref, n_ref, g_ref, x_out_ref, xs_ref, gz_ref, gx_ref):
    ant = h_ref.shape[-1]
    tiles = ant // 128
    top = top_mask((8, 128), 0)
    top_a = top_mask((8, ant), 0)
    chunk = DETECT_UNROLL

    def wide(x):
        return jnp.concatenate([x] * tiles, 1) if tiles > 1 else x

    def forward(get):
        def body(i, c):
            c = list(c)
            for k in range(chunk):
                u = i * chunk + k
                h = h_ref[u]
                x = get(u)
                j = 2 * (k % 4)
                c[j] = c[j] + h * wide(x)
                c[j + 1] = c[j + 1] + h * wide(swap_halves(x))
            return tuple(c)

        zero = jnp.zeros((8, ant), jnp.float32)
        c = lax.fori_loop(0, users // chunk, body, (zero,) * 8)
        a = (c[0] + c[2]) + (c[4] + c[6])
        b = (c[1] + c[3]) + (c[5] + c[7])
        return jnp.where(top_a, a - swap_halves(a), b + swap_halves(b))

    def adjoint(e, put):
        es = swap_halves(e)

        def body(i, c):
            for k in range(chunk):
                u = i * chunk + k
                h = h_ref[u]
                m, q = h * e, h * es
                m = sum(m[:, 128 * t : 128 * t + 128] for t in range(tiles))
                q = sum(q[:, 128 * t : 128 * t + 128] for t in range(tiles))
                v = jnp.where(top, m + swap_halves(m), swap_halves(q) - q)
                put(u, jnp.broadcast_to(jnp.sum(v, 1, keepdims=True), (8, 128)))
            return c

        lax.fori_loop(0, users // chunk, body, 0)

    y = forward(lambda u: s_ref[u]) + n_ref[...]
    errs = []
    for layer in range(LAYERS):
        e = y if layer == 0 else y - forward(lambda u: xs_ref[layer, u])
        errs.append(e)
        step = s_ref[users + layer]

        def put(u, v):
            z = step * v if layer == 0 else xs_ref[layer, u] + step * v
            xs_ref[layer + 1, u] = clip_level * jnp.tanh(z * (1.0 / clip_level))

        adjoint(e, put)

    x_out_ref[...] = xs_ref[LAYERS]
    backs = [None] * LAYERS
    for layer in reversed(range(LAYERS)):
        step = s_ref[users + layer]
        last = layer == LAYERS - 1

        def slope(i, c):
            for k in range(chunk):
                u = i * chunk + k
                x = xs_ref[layer + 1, u]
                gx = (x - s_ref[u]) * (2.0 / users) if last else gx_ref[u]
                t = x * (1.0 / clip_level)
                gz_ref[layer, u] = gx * (1.0 - t * t) * step
            return c

        lax.fori_loop(0, users // chunk, slope, 0)
        ge = forward(lambda u: gz_ref[layer, u])
        backs[layer] = ge
        if layer:
            def put(u, v):
                x = xs_ref[layer + 1, u]
                gx = (x - s_ref[u]) * (2.0 / users) if last else gx_ref[u]
                t = x * (1.0 / clip_level)
                gx_ref[u] = gx * (1.0 - t * t) - v

            adjoint(ge, put)

    sign = half_rows((8, ant), 0, 1.0, -1.0)
    pairs = [(v, sign * swap_halves(v)) for k in range(LAYERS) for v in (errs[k], backs[k])]

    def outer(u):
        s = s_ref[u]
        g = jnp.zeros((8, ant), jnp.float32)
        for k in range(LAYERS):
            for which in range(2):
                v, vs = pairs[2 * k + which]
                if which == 0:
                    b = gz_ref[k, u]
                else:
                    b = s - xs_ref[k, u] if k else s
                bs = swap_halves(b)
                g = g + v * wide(jnp.where(top, b, bs)) + vs * wide(jnp.where(top, bs, b))
        g_ref[u] = g

    def body(i, c):
        for k in range(4):
            outer(i * 4 + k)
        return c

    lax.fori_loop(0, users // 4, body, 0)


def detect(channel, symbols, noise):
    users, _, ant = channel.shape
    return pl.pallas_call(
        functools.partial(detect_kernel, users),
        in_specs=[
            pl.BlockSpec(memory_space=pltpu.VMEM),
            pl.BlockSpec(memory_space=pltpu.VMEM),
            pl.BlockSpec(memory_space=pltpu.VMEM),
        ],
        out_specs=[pl.BlockSpec(memory_space=pltpu.VMEM), pl.BlockSpec(memory_space=pltpu.VMEM)],
        out_shape=[
            jax.ShapeDtypeStruct((users, 8, ant), jnp.float32),
            jax.ShapeDtypeStruct((users, 8, 128), jnp.float32),
        ],
        scratch_shapes=[
            pltpu.VMEM((LAYERS + 1, users, 8, 128), jnp.float32),
            pltpu.VMEM((LAYERS, users, 8, 128), jnp.float32),
            pltpu.VMEM((users, 8, 128), jnp.float32),
        ],
        compiler_params=pltpu.CompilerParams(vmem_limit_bytes=16 << 20),
        name="detect",
    )(channel, symbols, noise)


def grad_kernel(n, ul, pw, per, unroll, g_ref, e_ref, x_ref, out_ref, w_ref, lhs_ref, mat_ref):
    u = pl.program_id(0)
    step = pl.program_id(1)
    parts = pw // 128
    ant = g_ref.shape[-1]
    half = ant // 2
    rows = lhs_ref.shape[0]

    @pl.when((u == 0) & (step == 0))
    def _():
        mat_ref[...] = jnp.zeros_like(mat_ref)

    @pl.when(step == 0)
    def _():
        plus = g_ref[:, 0, :, pl.ds(0, half)]
        minus = g_ref[:, 0, :, pl.ds(half, half)]
        odd = swap_halves(plus - minus) * half_rows(plus.shape, 1, -1.0, 1.0)
        mix = jnp.concatenate([plus + minus, odd], 2).reshape(rows, ant)
        high, low = split(mix)
        lhs_ref[:, pl.ds(0, ant)] = high
        lhs_ref[:, pl.ds(ant, ant)] = low

    sign = half_rows((8, pw), 0, 1.0, -1.0)
    kinds = lax.broadcasted_iota(jnp.int32, (MAT, pw), 0).astype(jnp.float32)

    def tile(i, slot):
        s = step * per + i
        fine = e_ref[0, i, pl.ds(rows, 16), :]
        coarse = e_ref[0, i, pl.ds(rows + 16, ant // 16), :]
        steering(fine, coarse, w_ref, slot)
        w_high = w_ref[slot, pl.ds(0, ant), :]
        w_low = w_ref[slot, pl.ds(ant, ant), :]
        l_high = lhs_ref[:, pl.ds(0, ant)]
        left = jnp.concatenate([l_high, lhs_ref[:, pl.ds(ant, ant)]], 0)
        pair = jnp.dot(left, w_high, preferred_element_type=jnp.float32)
        rest = jnp.dot(l_high, w_low, preferred_element_type=jnp.float32)
        q = (pair[:rows] + (pair[rows:] + rest)).reshape(rows // 8, 8, pw)
        e = e_ref[0, i, pl.ds(0, rows), :].reshape(rows // 8, 8, pw)
        a = jnp.sum(e * q, 0)
        b = jnp.sum(swap_halves(e) * q, 0)
        p_re = jnp.sum(a * sign, 0, keepdims=True)
        p_im = jnp.sum(b, 0, keepdims=True)
        for t in range(parts):
            lanes = slice(128 * t, 128 * t + 128)
            out_ref[s, pl.ds(t * ul + u, 1), :] = p_re[:, lanes]
            out_ref[s, pl.ds((parts + t) * ul + u, 1), :] = p_im[:, lanes]
        g_re, g_im, mat = (field_row(x_ref, parts, ul, s, j, u) for j in (2, 3, 4))
        along_re = g_re * p_re + g_im * p_im
        along_im = g_re * p_im - g_im * p_re
        hit = jnp.broadcast_to(mat, (MAT, pw)) == kinds
        mat_ref[0] += jnp.where(hit, jnp.broadcast_to(along_re, (MAT, pw)), 0.0)
        mat_ref[1] += jnp.where(hit, jnp.broadcast_to(along_im, (MAT, pw)), 0.0)

    def group(i, carry):
        for slot in range(unroll):
            tile(i * unroll + slot, slot)
        return carry

    lax.fori_loop(0, per // unroll, group, 0)

    @pl.when((u == ul - 1) & (step == n // per - 1))
    def _():
        lane = lax.broadcasted_iota(jnp.int32, (MAT, 128), 1)
        kind = lax.broadcasted_iota(jnp.int32, (MAT, 128), 0)
        line = jnp.zeros((1, 128), jnp.float32)
        for j in range(2):
            total = jnp.broadcast_to(jnp.sum(mat_ref[j], 1, keepdims=True), (MAT, 128))
            spread = jnp.where(lane == kind + j * MAT, total, 0.0)
            line = line + jnp.sum(spread, 0, keepdims=True)
        for s in range(n):
            out_ref[s, pl.ds(2 * parts * ul, 1), :] = line


def gradient(grads, kept, params):
    n, ul, _, ant = grads.shape
    wide = params.shape[1]
    pw = kept.shape[-1]
    rows = 8 * n
    sent = 2 * ul * (pw // 128) + 1
    per = n // GRAD_STEPS if n % GRAD_STEPS == 0 else n
    unroll = math.gcd(per, GRAD_UNROLL)
    return pl.pallas_call(
        functools.partial(grad_kernel, n, ul, pw, per, unroll),
        grid=(ul, n // per),
        in_specs=[
            pl.BlockSpec((n, 1, 8, ant), lambda u, j: (0, u, 0, 0)),
            pl.BlockSpec((1, per, kept.shape[2], pw), lambda u, j: (u, j, 0, 0)),
            pl.BlockSpec((n, wide, 128), lambda u, j: (0, 0, 0)),
        ],
        out_specs=pl.BlockSpec((n, sent, 128), lambda u, j: (0, 0, 0)),
        out_shape=jax.ShapeDtypeStruct((n, sent, 128), jnp.float32),
        scratch_shapes=[
            pltpu.VMEM((unroll, 2 * ant, pw), jnp.bfloat16),
            pltpu.VMEM((rows, 2 * ant), jnp.bfloat16),
            pltpu.VMEM((2, MAT, pw), jnp.float32),
        ],
        compiler_params=pltpu.CompilerParams(vmem_limit_bytes=GRAD_VMEM),
        name="gradient",
    )(grads, kept, params)


def unpack_kernel(n, ul, x_ref, grad_ref, mat_ref):
    parts = grad_ref.shape[-1] // 128
    total = x_ref[0, pl.ds(2 * parts * ul, 1), :]
    for s in range(1, n):
        total = total + x_ref[s, pl.ds(2 * parts * ul, 1), :]
    for j in range(2):
        mat_ref[pl.ds(j, 1), :] = total[:, j * MAT : j * MAT + MAT]
    for s in range(n):
        for j in range(2):
            for t in range(parts):
                rows = x_ref[s, pl.ds((j * parts + t) * ul, ul), :]
                grad_ref[j, pl.ds(s * ul, ul), pl.ds(128 * t, 128)] = rows


def unpack(received, users, pw):
    n = received.shape[0]
    return pl.pallas_call(
        functools.partial(unpack_kernel, n, users // n),
        in_specs=[pl.BlockSpec(memory_space=pltpu.VMEM)],
        out_specs=[pl.BlockSpec(memory_space=pltpu.VMEM)] * 2,
        out_shape=[
            jax.ShapeDtypeStruct((2, users, pw), jnp.float32),
            jax.ShapeDtypeStruct((2, MAT), jnp.float32),
        ],
        compiler_params=pltpu.CompilerParams(vmem_limit_bytes=8 << 20),
        name="unpack",
    )(received)


def antenna_order(ant):
    half = ant // 2
    offset = np.arange(half).reshape(-1, 2, 8)
    offset = np.stack([offset[:, 1], offset[:, 0, ::-1]], 1).reshape(half)
    return np.concatenate([half + offset, half - 1 - offset])


def exchange(x):
    return lax.all_to_all(x, "path", 0, 0, tiled=True)


def local(
    n,
    path_angle,
    path_delay,
    path_gain,
    material_ids,
    reflection,
    step_sizes,
    tone_ids,
    symbol_ids,
    receiver_noise,
):
    users, pw = path_angle.shape
    own, _, ant = receiver_noise.shape
    assert 2 * own == 8
    ul = users // n
    params = exchange(pack(n, path_angle, path_delay, path_gain, material_ids))
    tone = tone_ids.astype(jnp.float32) * (1.0 / TONE_SPAN)
    tone = jnp.broadcast_to(tone.reshape(n, 1, own), (n, 2, own)).reshape(8 * n)
    mirror = jnp.broadcast_to(reflection.T[:, :, None], (MAT, 2, 4)).reshape(8 * MAT)
    aux = jnp.concatenate([tone, mirror])
    aux = jnp.broadcast_to(aux[:, None], (8 * (n + MAT), 128))
    channel_rows, kept = synthesize(params, aux, ul, pw, ant)
    channel = exchange(channel_rows).reshape(users, 8, ant)

    symbols = jnp.stack([symbol_ids % 4, symbol_ids // 4], 0)
    symbols = (2 * symbols - 3).astype(jnp.float32) * qam_scale
    symbols = jnp.transpose(symbols, (2, 0, 1)).reshape(users, 8)
    symbols = jnp.concatenate([symbols, jnp.broadcast_to(step_sizes[:, None], (LAYERS, 8))], 0)
    symbols = jnp.broadcast_to(symbols[:, :, None], (users + LAYERS, 8, 128))
    noise = jnp.transpose(receiver_noise, (1, 0, 2)).reshape(8, ant)
    order = jnp.asarray(antenna_order(ant), jnp.int32)
    place = (order[None] == jnp.arange(ant, dtype=jnp.int32)[:, None]).astype(jnp.float32)
    noise = jnp.dot(noise, place, precision=lax.Precision.HIGHEST)
    grads, found = detect(channel, symbols, noise)
    estimates = jnp.transpose(found[:, :, 0].reshape(users, 2, own), (2, 1, 0))

    grads = exchange(grads.reshape(n, ul, 8, ant))
    sent = gradient(grads, kept, params)
    back = exchange(sent)
    path_grad, material_grad = unpack(back, users, pw)

    responses = jnp.transpose(channel.reshape(users, 2, own, ant), (2, 1, 0, 3))
    responses = jnp.einsum("...k,ak->...a", responses, place, precision=lax.Precision.HIGHEST)
    return (path_grad, estimates, material_grad, responses)


def solution(mesh):
    in_specs = (
        P(None, ("groups", "path")),
        P(None, ("groups", "path")),
        P(None, None, ("groups", "path")),
        P(None, ("groups", "path")),
        P(),
        P(),
        P("groups"),
        P(("groups", "path"), None),
        P(("groups", "path"), None, None),
    )
    out_specs = (
        P(None, None, ("groups", "path")),
        P(("groups", "path"), None, None),
        P(None, "groups"),
        P(("groups", "path"), None, None, None),
    )
    body = functools.partial(local, mesh.shape["path"])
    return jax.shard_map(body, mesh=mesh, in_specs=in_specs, out_specs=out_specs, check_vma=False)
```

```python
import functools
import math

import jax
import jax.numpy as jnp
import numpy as np
from jax import lax
from jax.experimental import pallas as pl
from jax.experimental.pallas import tpu as pltpu
from jax.sharding import PartitionSpec as P

MAT = 16
TONE_SPAN = 3276
LAYERS = 4
FIELDS = 5

SYNTH_VMEM = 48 << 20
GRAD_VMEM = 48 << 20
SYNTH_UNROLL = 16
SYNTH_JOINED = 16
GRAD_UNROLL = 16
DETECT_UNROLL = 64
GRAD_STEPS = 1

clip_level = 1.5
qam_scale = 1.0 / math.sqrt(10.0)

SINE = (
    6.283185160088971,
    -41.341655031286386,
    81.60100406453228,
    -76.5497820808334,
    39.536704364112744,
)


def cos_turns(t):
    a = 0.25 - jnp.abs(t - jnp.round(t))
    z = a * a
    p = SINE[4] * z + SINE[3]
    p = p * z + SINE[2]
    p = p * z + SINE[1]
    p = p * z + SINE[0]
    return p * a


RISE = (
    -0.16666660462354993,
    0.00833308816681783,
    -0.00019811112712181806,
    2.6089325665533767e-06,
)


def sine(angle):
    t = jnp.abs(angle)
    y = jnp.where(t > 0.5 * math.pi, (3.140625 - t) + (math.pi - 3.140625), t)
    z = y * y
    p = RISE[3] * z + RISE[2]
    p = p * z + RISE[1]
    p = p * z + RISE[0]
    s = y + (y * z) * p
    return jnp.where(angle < 0.0, -s, s)


def swap_halves(x):
    return pltpu.roll(x, 4, x.ndim - 2)


def half_rows(shape, dim, top, bottom):
    row = lax.broadcasted_iota(jnp.int32, shape, dim)
    return jnp.where(row % 8 < 4, jnp.float32(top), jnp.float32(bottom))


def top_mask(shape, dim):
    return lax.broadcasted_iota(jnp.int32, shape, dim) % 8 < 4


def split(x):
    high = x.astype(jnp.bfloat16)
    low = (x - high.astype(jnp.float32)).astype(jnp.bfloat16)
    return high, low


def pack_kernel(n, ul, angle_ref, delay_ref, gain_ref, ids_ref, out_ref):
    pw = angle_ref.shape[-1]
    fields = (
        0.5 * sine(angle_ref[...]),
        delay_ref[...],
        gain_ref[0],
        gain_ref[1],
        ids_ref[...].astype(jnp.float32),
    )
    parts = pw // 128
    for j, field in enumerate(fields):
        for t in range(parts):
            block = field[:, 128 * t : 128 * t + 128]
            for d in range(n):
                start = (j * parts + t) * ul
                out_ref[d, pl.ds(start, ul), :] = block[d * ul : d * ul + ul]


def pack(n, angle, delay, gain, ids):
    users, pw = angle.shape
    ul = users // n
    rows = FIELDS * ul * (pw // 128)
    return pl.pallas_call(
        functools.partial(pack_kernel, n, ul),
        in_specs=[pl.BlockSpec(memory_space=pltpu.VMEM)] * 4,
        out_specs=pl.BlockSpec(memory_space=pltpu.VMEM),
        out_shape=jax.ShapeDtypeStruct((n, rows, 128), jnp.float32),
        compiler_params=pltpu.CompilerParams(vmem_limit_bytes=60 << 20),
        name="pack",
    )(angle, delay, gain, ids)


def field_row(x_ref, parts, ul, s, j, u):
    rows = [x_ref[s, pl.ds((j * parts + t) * ul + u, 1), :] for t in range(parts)]
    return jnp.concatenate(rows, 1)


def steering(fine, coarse, w_ref, slot):
    blocks = coarse.shape[0] // 2
    half = 16 * blocks
    f_cos, f_sin = fine[:8], fine[8:]
    for b in range(blocks):
        c_cos = coarse[b : b + 1]
        c_sin = coarse[blocks + b : blocks + b + 1]
        cc, ss = c_cos * f_cos, c_sin * f_sin
        sc, cs = c_sin * f_cos, c_cos * f_sin
        a_cos = jnp.concatenate([cc - ss, cc + ss], 0)
        a_sin = jnp.concatenate([sc + cs, sc - cs], 0)
        for base, val in ((0, a_cos), (half, a_sin)):
            high, low = split(val)
            w_ref[slot, pl.ds(base + 16 * b, 16), :] = high
            w_ref[slot, pl.ds(2 * half + base + 16 * b, 16), :] = low


def synth_kernel(n, ul, pw, unroll, x_ref, aux_ref, h_ref, e_ref, w_ref, lhs_ref, acc_ref, c_ref):
    u = pl.program_id(0)
    parts = pw // 128
    half = acc_ref.shape[-1] // 2
    rows = acc_ref.shape[0]
    top8 = top_mask((8, pw), 0)
    shift8 = half_rows((8, pw), 0, 0.0, -0.25)
    blocks = half // 16
    fine_row = lax.broadcasted_iota(jnp.int32, (16, pw), 0)
    fine_coef = (fine_row % 8).astype(jnp.float32) + 0.5
    fine_shift = jnp.where(fine_row < 8, 0.0, -0.25)
    coarse_row = lax.broadcasted_iota(jnp.int32, (2 * blocks, pw), 0)
    coarse_coef = (coarse_row % blocks).astype(jnp.float32) * 16.0 + 8.0
    coarse_shift = jnp.where(coarse_row < blocks, 0.0, -0.25)

    def coefficients():
        def column(j):
            return jnp.concatenate([field_row(x_ref, parts, ul, s, j, u) for s in range(n)], 0)

        def wide(r):
            line = jnp.broadcast_to(aux_ref[pl.ds(rows + r, 1), :], (n, 128))
            return jnp.concatenate([line] * parts, 1)

        g_re, g_im, mat = (column(j) for j in (2, 3, 4))
        mat = mat.astype(jnp.int32)
        bits = [(mat & (1 << bit)) != 0 for bit in range(MAT.bit_length() - 1)]
        refl = []
        for base in (0, MAT):
            level = [wide(base + m) for m in range(MAT)]
            for hit in bits:
                level = [jnp.where(hit, y, x) for x, y in zip(level[::2], level[1::2])]
            refl.append(level[0])
        c_ref[0] = g_re * refl[0] - g_im * refl[1]
        c_ref[1] = g_re * refl[1] + g_im * refl[0]

    def tile(s, slot):
        w, dly = (field_row(x_ref, parts, ul, s, j, u) for j in range(2))
        w8 = jnp.broadcast_to(w, (8, pw))
        fine = cos_turns(fine_coef * jnp.concatenate([w8] * 2, 0) + fine_shift)
        w16 = jnp.concatenate([w8] * (2 * blocks // 8), 0)
        coarse = cos_turns(coarse_coef * w16 + coarse_shift)
        e_ref[0, s, pl.ds(rows, 16), :] = fine
        e_ref[0, s, pl.ds(rows + 16, 2 * blocks), :] = coarse
        steering(fine, coarse, w_ref, slot)
        c_re = jnp.broadcast_to(c_ref[0, pl.ds(s, 1), :], (8, pw))
        c_im = jnp.broadcast_to(c_ref[1, pl.ds(s, 1), :], (8, pw))
        c_mix = jnp.where(top8, c_re, -c_re)
        centre = w * (half - 0.5)
        centre = centre - jnp.round(centre)
        base8 = shift8 + centre
        d8 = jnp.broadcast_to(dly, (8, pw))
        step = 32
        for q in range(rows // step):
            rq = pl.ds(q * step, step)
            tone = aux_ref[rq, :]
            tone = jnp.concatenate([tone] * parts, 1)
            d32 = jnp.concatenate([d8] * (step // 8), 0)
            b32 = jnp.concatenate([base8] * (step // 8), 0)
            e = cos_turns(tone * d32 + b32)
            e_ref[0, s, rq, :] = e
            e3 = e.reshape(step // 8, 8, pw)
            g = e3 * c_mix[None] + swap_halves(e3) * c_im[None]
            high, low = split(g.reshape(step, pw))
            lhs_ref[slot, rq, pl.ds(0, pw)] = high
            lhs_ref[slot, rq, pl.ds(pw, pw)] = low

    def product(slots):
        def lhs(base):
            return jnp.concatenate([lhs_ref[k, :, pl.ds(base, pw)] for k in slots], 1)

        def steer(base):
            return jnp.concatenate([w_ref[k, pl.ds(base, 2 * half), :] for k in slots], 1)

        dims = (((1,), (1,)), ((), ()))
        l_high = lhs(0)
        left = jnp.concatenate([l_high, lhs(pw)], 0)
        pair = lax.dot_general(left, steer(0), dims, preferred_element_type=jnp.float32)
        rest = lax.dot_general(l_high, steer(2 * half), dims, preferred_element_type=jnp.float32)
        acc_ref[...] += pair[:rows] + (pair[rows:] + rest)

    joined = math.gcd(unroll, SYNTH_JOINED)

    def group(i, carry):
        for first in range(0, unroll, joined):
            slots = range(first, first + joined)
            for slot in slots:
                tile(i * unroll + slot, slot)
            product(slots)
        return carry

    coefficients()
    acc_ref[...] = jnp.zeros_like(acc_ref)
    lax.fori_loop(0, n // unroll, group, 0)
    even = acc_ref[:, pl.ds(0, half)].reshape(rows // 8, 8, half)
    odd = acc_ref[:, pl.ds(half, half)].reshape(rows // 8, 8, half)
    odd = swap_halves(odd) * half_rows(odd.shape, 1, 1.0, -1.0)
    h_ref[:, 0, :, pl.ds(0, half)] = even + odd
    h_ref[:, 0, :, pl.ds(half, half)] = even - odd


def synthesize(params, aux, ul, pw, antennas):
    n, wide, _ = params.shape
    rows = 8 * n
    kept = rows + 16 + antennas // 16
    unroll = math.gcd(n, SYNTH_UNROLL)
    return pl.pallas_call(
        functools.partial(synth_kernel, n, ul, pw, unroll),
        grid=(ul,),
        in_specs=[
            pl.BlockSpec((n, wide, 128), lambda u: (0, 0, 0)),
            pl.BlockSpec(aux.shape, lambda u: (0, 0)),
        ],
        out_specs=[
            pl.BlockSpec((n, 1, 8, antennas), lambda u: (0, u, 0, 0)),
            pl.BlockSpec((1, n, kept, pw), lambda u: (u, 0, 0, 0)),
        ],
        out_shape=[
            jax.ShapeDtypeStruct((n, ul, 8, antennas), jnp.float32),
            jax.ShapeDtypeStruct((ul, n, kept, pw), jnp.float32),
        ],
        scratch_shapes=[
            pltpu.VMEM((unroll, 2 * antennas, pw), jnp.bfloat16),
            pltpu.VMEM((unroll, rows, 2 * pw), jnp.bfloat16),
            pltpu.VMEM((rows, antennas), jnp.float32),
            pltpu.VMEM((2, n, pw), jnp.float32),
        ],
        compiler_params=pltpu.CompilerParams(vmem_limit_bytes=SYNTH_VMEM),
        name="synth",
    )(params, aux)


def detect_kernel(users, h_ref, s_ref, n_ref, g_ref, x_out_ref, xs_ref, gz_ref, gx_ref):
    ant = h_ref.shape[-1]
    tiles = ant // 128
    top = top_mask((8, 128), 0)
    top_a = top_mask((8, ant), 0)
    chunk = DETECT_UNROLL

    def wide(x):
        return jnp.concatenate([x] * tiles, 1) if tiles > 1 else x

    def forward(get):
        def body(i, c):
            c = list(c)
            for k in range(chunk):
                u = i * chunk + k
                h = h_ref[u]
                x = get(u)
                j = 2 * (k % 4)
                c[j] = c[j] + h * wide(x)
                c[j + 1] = c[j + 1] + h * wide(swap_halves(x))
            return tuple(c)

        zero = jnp.zeros((8, ant), jnp.float32)
        c = lax.fori_loop(0, users // chunk, body, (zero,) * 8)
        a = (c[0] + c[2]) + (c[4] + c[6])
        b = (c[1] + c[3]) + (c[5] + c[7])
        return jnp.where(top_a, a - swap_halves(a), b + swap_halves(b))

    def adjoint(e, put):
        es = swap_halves(e)

        def body(i, c):
            for k in range(chunk):
                u = i * chunk + k
                h = h_ref[u]
                m, q = h * e, h * es
                m = sum(m[:, 128 * t : 128 * t + 128] for t in range(tiles))
                q = sum(q[:, 128 * t : 128 * t + 128] for t in range(tiles))
                v = jnp.where(top, m + swap_halves(m), swap_halves(q) - q)
                put(u, jnp.broadcast_to(jnp.sum(v, 1, keepdims=True), (8, 128)))
            return c

        lax.fori_loop(0, users // chunk, body, 0)

    y = forward(lambda u: s_ref[u]) + n_ref[...]
    errs = []
    for layer in range(LAYERS):
        e = y if layer == 0 else y - forward(lambda u: xs_ref[layer, u])
        errs.append(e)
        step = s_ref[users + layer]

        def put(u, v):
            z = step * v if layer == 0 else xs_ref[layer, u] + step * v
            xs_ref[layer + 1, u] = clip_level * jnp.tanh(z * (1.0 / clip_level))

        adjoint(e, put)

    x_out_ref[...] = xs_ref[LAYERS]
    backs = [None] * LAYERS
    for layer in reversed(range(LAYERS)):
        step = s_ref[users + layer]
        last = layer == LAYERS - 1

        def slope(i, c):
            for k in range(chunk):
                u = i * chunk + k
                x = xs_ref[layer + 1, u]
                gx = (x - s_ref[u]) * (2.0 / users) if last else gx_ref[u]
                t = x * (1.0 / clip_level)
                gz_ref[layer, u] = gx * (1.0 - t * t) * step
            return c

        lax.fori_loop(0, users // chunk, slope, 0)
        ge = forward(lambda u: gz_ref[layer, u])
        backs[layer] = ge
        if layer:
            def put(u, v):
                x = xs_ref[layer + 1, u]
                gx = (x - s_ref[u]) * (2.0 / users) if last else gx_ref[u]
                t = x * (1.0 / clip_level)
                gx_ref[u] = gx * (1.0 - t * t) - v

            adjoint(ge, put)

    sign = half_rows((8, ant), 0, 1.0, -1.0)
    pairs = [(v, sign * swap_halves(v)) for k in range(LAYERS) for v in (errs[k], backs[k])]

    def outer(u):
        s = s_ref[u]
        g = jnp.zeros((8, ant), jnp.float32)
        for k in range(LAYERS):
            for which in range(2):
                v, vs = pairs[2 * k + which]
                if which == 0:
                    b = gz_ref[k, u]
                else:
                    b = s - xs_ref[k, u] if k else s
                bs = swap_halves(b)
                g = g + v * wide(jnp.where(top, b, bs)) + vs * wide(jnp.where(top, bs, b))
        g_ref[u] = g

    def body(i, c):
        for k in range(4):
            outer(i * 4 + k)
        return c

    lax.fori_loop(0, users // 4, body, 0)


def detect(channel, symbols, noise):
    users, _, ant = channel.shape
    return pl.pallas_call(
        functools.partial(detect_kernel, users),
        in_specs=[
            pl.BlockSpec(memory_space=pltpu.VMEM),
            pl.BlockSpec(memory_space=pltpu.VMEM),
            pl.BlockSpec(memory_space=pltpu.VMEM),
        ],
        out_specs=[pl.BlockSpec(memory_space=pltpu.VMEM), pl.BlockSpec(memory_space=pltpu.VMEM)],
        out_shape=[
            jax.ShapeDtypeStruct((users, 8, ant), jnp.float32),
            jax.ShapeDtypeStruct((users, 8, 128), jnp.float32),
        ],
        scratch_shapes=[
            pltpu.VMEM((LAYERS + 1, users, 8, 128), jnp.float32),
            pltpu.VMEM((LAYERS, users, 8, 128), jnp.float32),
            pltpu.VMEM((users, 8, 128), jnp.float32),
        ],
        compiler_params=pltpu.CompilerParams(vmem_limit_bytes=16 << 20),
        name="detect",
    )(channel, symbols, noise)


def grad_kernel(n, ul, pw, per, unroll, g_ref, e_ref, x_ref, out_ref, w_ref, lhs_ref, mat_ref):
    u = pl.program_id(0)
    step = pl.program_id(1)
    parts = pw // 128
    ant = g_ref.shape[-1]
    half = ant // 2
    rows = lhs_ref.shape[0]

    @pl.when((u == 0) & (step == 0))
    def _():
        mat_ref[...] = jnp.zeros_like(mat_ref)

    @pl.when(step == 0)
    def _():
        plus = g_ref[:, 0, :, pl.ds(0, half)]
        minus = g_ref[:, 0, :, pl.ds(half, half)]
        odd = swap_halves(plus - minus) * half_rows(plus.shape, 1, -1.0, 1.0)
        mix = jnp.concatenate([plus + minus, odd], 2).reshape(rows, ant)
        high, low = split(mix)
        lhs_ref[:, pl.ds(0, ant)] = high
        lhs_ref[:, pl.ds(ant, ant)] = low

    sign = half_rows((8, pw), 0, 1.0, -1.0)
    kinds = lax.broadcasted_iota(jnp.int32, (MAT, pw), 0).astype(jnp.float32)

    def tile(i, slot):
        s = step * per + i
        fine = e_ref[0, i, pl.ds(rows, 16), :]
        coarse = e_ref[0, i, pl.ds(rows + 16, ant // 16), :]
        steering(fine, coarse, w_ref, slot)
        w_high = w_ref[slot, pl.ds(0, ant), :]
        w_low = w_ref[slot, pl.ds(ant, ant), :]
        l_high = lhs_ref[:, pl.ds(0, ant)]
        left = jnp.concatenate([l_high, lhs_ref[:, pl.ds(ant, ant)]], 0)
        pair = jnp.dot(left, w_high, preferred_element_type=jnp.float32)
        rest = jnp.dot(l_high, w_low, preferred_element_type=jnp.float32)
        q = (pair[:rows] + (pair[rows:] + rest)).reshape(rows // 8, 8, pw)
        e = e_ref[0, i, pl.ds(0, rows), :].reshape(rows // 8, 8, pw)
        a = jnp.sum(e * q, 0)
        b = jnp.sum(swap_halves(e) * q, 0)
        p_re = jnp.sum(a * sign, 0, keepdims=True)
        p_im = jnp.sum(b, 0, keepdims=True)
        for t in range(parts):
            lanes = slice(128 * t, 128 * t + 128)
            out_ref[s, t * ul + u] = p_re[:, lanes]
            out_ref[s, (parts + t) * ul + u] = p_im[:, lanes]
        g_re, g_im, mat = (field_row(x_ref, parts, ul, s, j, u) for j in (2, 3, 4))
        along_re = g_re * p_re + g_im * p_im
        along_im = g_re * p_im - g_im * p_re
        hit = jnp.broadcast_to(mat, (MAT, pw)) == kinds
        mat_ref[0] += jnp.where(hit, jnp.broadcast_to(along_re, (MAT, pw)), 0.0)
        mat_ref[1] += jnp.where(hit, jnp.broadcast_to(along_im, (MAT, pw)), 0.0)

    def group(i, carry):
        for slot in range(unroll):
            tile(i * unroll + slot, slot)
        return carry

    lax.fori_loop(0, per // unroll, group, 0)

    @pl.when((u == ul - 1) & (step == n // per - 1))
    def _():
        lane = lax.broadcasted_iota(jnp.int32, (MAT, 128), 1)
        kind = lax.broadcasted_iota(jnp.int32, (MAT, 128), 0)
        line = jnp.zeros((1, 128), jnp.float32)
        for j in range(2):
            total = jnp.broadcast_to(jnp.sum(mat_ref[j], 1, keepdims=True), (MAT, 128))
            spread = jnp.where(lane == kind + j * MAT, total, 0.0)
            line = line + jnp.sum(spread, 0, keepdims=True)
        for s in range(n):
            out_ref[s, 2 * parts * ul] = line


def gradient(grads, kept, params):
    n, ul, _, ant = grads.shape
    wide = params.shape[1]
    pw = kept.shape[-1]
    rows = 8 * n
    sent = 2 * ul * (pw // 128) + 1
    per = n // GRAD_STEPS if n % GRAD_STEPS == 0 else n
    unroll = math.gcd(per, GRAD_UNROLL)
    return pl.pallas_call(
        functools.partial(grad_kernel, n, ul, pw, per, unroll),
        grid=(ul, n // per),
        in_specs=[
            pl.BlockSpec((n, 1, 8, ant), lambda u, j: (0, u, 0, 0)),
            pl.BlockSpec((1, per, kept.shape[2], pw), lambda u, j: (u, j, 0, 0)),
            pl.BlockSpec((n, wide, 128), lambda u, j: (0, 0, 0)),
        ],
        out_specs=pl.BlockSpec((n, sent, 1, 128), lambda u, j: (0, 0, 0, 0)),
        out_shape=jax.ShapeDtypeStruct((n, sent, 1, 128), jnp.float32),
        scratch_shapes=[
            pltpu.VMEM((unroll, 2 * ant, pw), jnp.bfloat16),
            pltpu.VMEM((rows, 2 * ant), jnp.bfloat16),
            pltpu.VMEM((2, MAT, pw), jnp.float32),
        ],
        compiler_params=pltpu.CompilerParams(vmem_limit_bytes=GRAD_VMEM),
        name="gradient",
    )(grads, kept, params)


def unpack_kernel(n, ul, x_ref, grad_ref, mat_ref):
    parts = grad_ref.shape[-1] // 128
    total = x_ref[0, 2 * parts * ul]
    for s in range(1, n):
        total = total + x_ref[s, 2 * parts * ul]
    for j in range(2):
        mat_ref[pl.ds(j, 1), :] = total[:, j * MAT : j * MAT + MAT]
    for s in range(n):
        for j in range(2):
            for t in range(parts):
                rows = [x_ref[s, (j * parts + t) * ul + k] for k in range(ul)]
                rows = jnp.concatenate(rows, 0)
                grad_ref[j, pl.ds(s * ul, ul), pl.ds(128 * t, 128)] = rows


def unpack(received, users, pw):
    n = received.shape[0]
    return pl.pallas_call(
        functools.partial(unpack_kernel, n, users // n),
        in_specs=[pl.BlockSpec(memory_space=pltpu.VMEM)],
        out_specs=[pl.BlockSpec(memory_space=pltpu.VMEM)] * 2,
        out_shape=[
            jax.ShapeDtypeStruct((2, users, pw), jnp.float32),
            jax.ShapeDtypeStruct((2, MAT), jnp.float32),
        ],
        compiler_params=pltpu.CompilerParams(vmem_limit_bytes=8 << 20),
        name="unpack",
    )(received)


def antenna_order(ant):
    half = ant // 2
    offset = np.arange(half).reshape(-1, 2, 8)
    offset = np.stack([offset[:, 1], offset[:, 0, ::-1]], 1).reshape(half)
    return np.concatenate([half + offset, half - 1 - offset])


def exchange(x):
    return lax.all_to_all(x, "path", 0, 0, tiled=True)


def local(
    n,
    path_angle,
    path_delay,
    path_gain,
    material_ids,
    reflection,
    step_sizes,
    tone_ids,
    symbol_ids,
    receiver_noise,
):
    users, pw = path_angle.shape
    own, _, ant = receiver_noise.shape
    assert 2 * own == 8
    ul = users // n
    params = exchange(pack(n, path_angle, path_delay, path_gain, material_ids))
    tone = tone_ids.astype(jnp.float32) * (1.0 / TONE_SPAN)
    tone = jnp.broadcast_to(tone.reshape(n, 1, own), (n, 2, own)).reshape(8 * n)
    aux = jnp.concatenate([tone, reflection.reshape(2 * MAT)])
    aux = jnp.broadcast_to(aux[:, None], (8 * n + 2 * MAT, 128))
    channel_rows, kept = synthesize(params, aux, ul, pw, ant)
    channel = exchange(channel_rows).reshape(users, 8, ant)

    symbols = jnp.stack([symbol_ids % 4, symbol_ids // 4], 0)
    symbols = (2 * symbols - 3).astype(jnp.float32) * qam_scale
    symbols = jnp.transpose(symbols, (2, 0, 1)).reshape(users, 8)
    symbols = jnp.concatenate([symbols, jnp.broadcast_to(step_sizes[:, None], (LAYERS, 8))], 0)
    symbols = jnp.broadcast_to(symbols[:, :, None], (users + LAYERS, 8, 128))
    noise = jnp.transpose(receiver_noise, (1, 0, 2)).reshape(8, ant)
    order = jnp.asarray(antenna_order(ant), jnp.int32)
    place = (order[None] == jnp.arange(ant, dtype=jnp.int32)[:, None]).astype(jnp.float32)
    noise = jnp.dot(noise, place, precision=lax.Precision.HIGHEST)
    grads, found = detect(channel, symbols, noise)
    estimates = jnp.transpose(found[:, :, 0].reshape(users, 2, own), (2, 1, 0))

    grads = exchange(grads.reshape(n, ul, 8, ant))
    sent = gradient(grads, kept, params)
    back = exchange(sent)
    path_grad, material_grad = unpack(back, users, pw)

    responses = jnp.transpose(channel.reshape(users, 2, own, ant), (2, 1, 0, 3))
    responses = jnp.einsum("...k,ak->...a", responses, place, precision=lax.Precision.HIGHEST)
    return (path_grad, estimates, material_grad, responses)


def solution(mesh):
    in_specs = (
        P(None, ("groups", "path")),
        P(None, ("groups", "path")),
        P(None, None, ("groups", "path")),
        P(None, ("groups", "path")),
        P(),
        P(),
        P("groups"),
        P(("groups", "path"), None),
        P(("groups", "path"), None, None),
    )
    out_specs = (
        P(None, None, ("groups", "path")),
        P(("groups", "path"), None, None),
        P(None, "groups"),
        P(("groups", "path"), None, None, None),
    )
    body = functools.partial(local, mesh.shape["path"])
    return jax.shard_map(body, mesh=mesh, in_specs=in_specs, out_specs=out_specs, check_vma=False)
```

```python
import functools
import math

import jax
import jax.numpy as jnp
import numpy as np
from jax import lax
from jax.experimental import pallas as pl
from jax.experimental.pallas import tpu as pltpu
from jax.sharding import PartitionSpec as P

MAT = 16
TONE_SPAN = 3276
LAYERS = 4
FIELDS = 5

SYNTH_VMEM = 48 << 20
GRAD_VMEM = 48 << 20
SYNTH_UNROLL = 16
SYNTH_JOINED = 16
GRAD_UNROLL = 16
DETECT_UNROLL = 64
GRAD_STEPS = 1

clip_level = 1.5
qam_scale = 1.0 / math.sqrt(10.0)

SINE = (
    6.283185160088971,
    -41.341655031286386,
    81.60100406453228,
    -76.5497820808334,
    39.536704364112744,
)


def cos_turns(t):
    a = 0.25 - jnp.abs(t - jnp.round(t))
    z = a * a
    p = SINE[4] * z + SINE[3]
    p = p * z + SINE[2]
    p = p * z + SINE[1]
    p = p * z + SINE[0]
    return p * a


RISE = (
    -0.16666660462354993,
    0.00833308816681783,
    -0.00019811112712181806,
    2.6089325665533767e-06,
)


def sine(angle):
    t = jnp.abs(angle)
    y = jnp.where(t > 0.5 * math.pi, (3.140625 - t) + (math.pi - 3.140625), t)
    z = y * y
    p = RISE[3] * z + RISE[2]
    p = p * z + RISE[1]
    p = p * z + RISE[0]
    s = y + (y * z) * p
    return jnp.where(angle < 0.0, -s, s)


def swap_halves(x):
    return pltpu.roll(x, 4, x.ndim - 2)


def half_rows(shape, dim, top, bottom):
    row = lax.broadcasted_iota(jnp.int32, shape, dim)
    return jnp.where(row % 8 < 4, jnp.float32(top), jnp.float32(bottom))


def top_mask(shape, dim):
    return lax.broadcasted_iota(jnp.int32, shape, dim) % 8 < 4


def split(x):
    high = x.astype(jnp.bfloat16)
    low = (x - high.astype(jnp.float32)).astype(jnp.bfloat16)
    return high, low


def pack_kernel(n, ul, angle_ref, delay_ref, gain_ref, ids_ref, out_ref):
    pw = angle_ref.shape[-1]
    fields = (
        0.5 * sine(angle_ref[...]),
        delay_ref[...],
        gain_ref[0],
        gain_ref[1],
        ids_ref[...].astype(jnp.float32),
    )
    parts = pw // 128
    for j, field in enumerate(fields):
        for t in range(parts):
            block = field[:, 128 * t : 128 * t + 128]
            for d in range(n):
                start = (j * parts + t) * ul
                out_ref[d, pl.ds(start, ul), :] = block[d * ul : d * ul + ul]


def pack(n, angle, delay, gain, ids):
    users, pw = angle.shape
    ul = users // n
    rows = FIELDS * ul * (pw // 128)
    return pl.pallas_call(
        functools.partial(pack_kernel, n, ul),
        in_specs=[pl.BlockSpec(memory_space=pltpu.VMEM)] * 4,
        out_specs=pl.BlockSpec(memory_space=pltpu.VMEM),
        out_shape=jax.ShapeDtypeStruct((n, rows, 128), jnp.float32),
        compiler_params=pltpu.CompilerParams(vmem_limit_bytes=60 << 20),
        name="pack",
    )(angle, delay, gain, ids)


def field_row(x_ref, parts, ul, s, j, u):
    rows = [x_ref[s, pl.ds((j * parts + t) * ul + u, 1), :] for t in range(parts)]
    return jnp.concatenate(rows, 1)


def steering(fine, coarse, w_ref, slot):
    blocks = coarse.shape[0] // 2
    half = 16 * blocks
    f_cos, f_sin = fine[:8], fine[8:]
    for b in range(blocks):
        c_cos = coarse[b : b + 1]
        c_sin = coarse[blocks + b : blocks + b + 1]
        cc, ss = c_cos * f_cos, c_sin * f_sin
        sc, cs = c_sin * f_cos, c_cos * f_sin
        a_cos = jnp.concatenate([cc - ss, cc + ss], 0)
        a_sin = jnp.concatenate([sc + cs, sc - cs], 0)
        for base, val in ((0, a_cos), (half, a_sin)):
            high, low = split(val)
            w_ref[slot, pl.ds(base + 16 * b, 16), :] = high
            w_ref[slot, pl.ds(2 * half + base + 16 * b, 16), :] = low


def synth_kernel(n, ul, pw, unroll, x_ref, aux_ref, h_ref, e_ref, w_ref, lhs_ref, acc_ref, c_ref):
    u = pl.program_id(0)
    parts = pw // 128
    half = acc_ref.shape[-1] // 2
    rows = acc_ref.shape[0]
    top8 = top_mask((8, pw), 0)
    shift8 = half_rows((8, pw), 0, 0.0, -0.25)
    blocks = half // 16
    fine_row = lax.broadcasted_iota(jnp.int32, (16, pw), 0)
    fine_coef = (fine_row % 8).astype(jnp.float32) + 0.5
    fine_shift = jnp.where(fine_row < 8, 0.0, -0.25)
    coarse_row = lax.broadcasted_iota(jnp.int32, (2 * blocks, pw), 0)
    coarse_coef = (coarse_row % blocks).astype(jnp.float32) * 16.0 + 8.0
    coarse_shift = jnp.where(coarse_row < blocks, 0.0, -0.25)

    def coefficients():
        def column(j):
            return jnp.concatenate([field_row(x_ref, parts, ul, s, j, u) for s in range(n)], 0)

        def wide(r):
            line = jnp.broadcast_to(aux_ref[pl.ds(rows + r, 1), :], (n, 128))
            return jnp.concatenate([line] * parts, 1)

        g_re, g_im, mat = (column(j) for j in (2, 3, 4))
        mat = mat.astype(jnp.int32)
        bits = [(mat & (1 << bit)) != 0 for bit in range(MAT.bit_length() - 1)]
        refl = []
        for base in (0, MAT):
            level = [wide(base + m) for m in range(MAT)]
            for hit in bits:
                level = [jnp.where(hit, y, x) for x, y in zip(level[::2], level[1::2])]
            refl.append(level[0])
        c_ref[0] = g_re * refl[0] - g_im * refl[1]
        c_ref[1] = g_re * refl[1] + g_im * refl[0]

    def tile(s, slot):
        w, dly = (field_row(x_ref, parts, ul, s, j, u) for j in range(2))
        w8 = jnp.broadcast_to(w, (8, pw))
        fine = cos_turns(fine_coef * jnp.concatenate([w8] * 2, 0) + fine_shift)
        w16 = jnp.concatenate([w8] * (2 * blocks // 8), 0)
        coarse = cos_turns(coarse_coef * w16 + coarse_shift)
        e_ref[0, s, pl.ds(rows, 16), :] = fine
        e_ref[0, s, pl.ds(rows + 16, 2 * blocks), :] = coarse
        steering(fine, coarse, w_ref, slot)
        c_re = jnp.broadcast_to(c_ref[0, pl.ds(s, 1), :], (8, pw))
        c_im = jnp.broadcast_to(c_ref[1, pl.ds(s, 1), :], (8, pw))
        c_mix = jnp.where(top8, c_re, -c_re)
        centre = w * (half - 0.5)
        centre = centre - jnp.round(centre)
        base8 = shift8 + centre
        d8 = jnp.broadcast_to(dly, (8, pw))
        step = 32
        for q in range(rows // step):
            rq = pl.ds(q * step, step)
            tone = aux_ref[rq, :]
            tone = jnp.concatenate([tone] * parts, 1)
            d32 = jnp.concatenate([d8] * (step // 8), 0)
            b32 = jnp.concatenate([base8] * (step // 8), 0)
            e = cos_turns(tone * d32 + b32)
            e_ref[0, s, rq, :] = e
            e3 = e.reshape(step // 8, 8, pw)
            g = e3 * c_mix[None] + swap_halves(e3) * c_im[None]
            high, low = split(g.reshape(step, pw))
            lhs_ref[slot, rq, pl.ds(0, pw)] = high
            lhs_ref[slot, rq, pl.ds(pw, pw)] = low

    def product(slots):
        def lhs(base):
            return jnp.concatenate([lhs_ref[k, :, pl.ds(base, pw)] for k in slots], 1)

        def steer(base):
            return jnp.concatenate([w_ref[k, pl.ds(base, 2 * half), :] for k in slots], 1)

        dims = (((1,), (1,)), ((), ()))
        l_high = lhs(0)
        left = jnp.concatenate([l_high, lhs(pw)], 0)
        pair = lax.dot_general(left, steer(0), dims, preferred_element_type=jnp.float32)
        rest = lax.dot_general(l_high, steer(2 * half), dims, preferred_element_type=jnp.float32)
        acc_ref[...] += pair[:rows] + (pair[rows:] + rest)

    joined = math.gcd(unroll, SYNTH_JOINED)

    def group(i, carry):
        for first in range(0, unroll, joined):
            slots = range(first, first + joined)
            for slot in slots:
                tile(i * unroll + slot, slot)
            product(slots)
        return carry

    coefficients()
    acc_ref[...] = jnp.zeros_like(acc_ref)
    lax.fori_loop(0, n // unroll, group, 0)
    even = acc_ref[:, pl.ds(0, half)].reshape(rows // 8, 8, half)
    odd = acc_ref[:, pl.ds(half, half)].reshape(rows // 8, 8, half)
    odd = swap_halves(odd) * half_rows(odd.shape, 1, 1.0, -1.0)
    h_ref[:, 0, :, pl.ds(0, half)] = even + odd
    h_ref[:, 0, :, pl.ds(half, half)] = even - odd


def synthesize(params, aux, ul, pw, antennas):
    n = params.shape[0]
    rows = 8 * n
    kept = rows + 16 + antennas // 16
    unroll = math.gcd(n, SYNTH_UNROLL)
    return pl.pallas_call(
        functools.partial(synth_kernel, n, ul, pw, unroll),
        grid=(ul,),
        in_specs=[
            pl.BlockSpec(memory_space=pltpu.VMEM),
            pl.BlockSpec(memory_space=pltpu.VMEM),
        ],
        out_specs=[
            pl.BlockSpec((n, 1, 8, antennas), lambda u: (0, u, 0, 0)),
            pl.BlockSpec((1, n, kept, pw), lambda u: (u, 0, 0, 0)),
        ],
        out_shape=[
            jax.ShapeDtypeStruct((n, ul, 8, antennas), jnp.float32),
            jax.ShapeDtypeStruct((ul, n, kept, pw), jnp.float32),
        ],
        scratch_shapes=[
            pltpu.VMEM((unroll, 2 * antennas, pw), jnp.bfloat16),
            pltpu.VMEM((unroll, rows, 2 * pw), jnp.bfloat16),
            pltpu.VMEM((rows, antennas), jnp.float32),
            pltpu.VMEM((2, n, pw), jnp.float32),
        ],
        compiler_params=pltpu.CompilerParams(vmem_limit_bytes=SYNTH_VMEM),
        name="synth",
    )(params, aux)


def detect_kernel(users, h_ref, s_ref, n_ref, g_ref, x_out_ref, xs_ref, gz_ref, gx_ref):
    ant = h_ref.shape[-1]
    tiles = ant // 128
    top = top_mask((8, 128), 0)
    top_a = top_mask((8, ant), 0)
    chunk = DETECT_UNROLL

    def wide(x):
        return jnp.concatenate([x] * tiles, 1) if tiles > 1 else x

    def forward(get):
        def body(i, c):
            c = list(c)
            for k in range(chunk):
                u = i * chunk + k
                h = h_ref[u]
                x = get(u)
                j = 2 * (k % 4)
                c[j] = c[j] + h * wide(x)
                c[j + 1] = c[j + 1] + h * wide(swap_halves(x))
            return tuple(c)

        zero = jnp.zeros((8, ant), jnp.float32)
        c = lax.fori_loop(0, users // chunk, body, (zero,) * 8)
        a = (c[0] + c[2]) + (c[4] + c[6])
        b = (c[1] + c[3]) + (c[5] + c[7])
        return jnp.where(top_a, a - swap_halves(a), b + swap_halves(b))

    def adjoint(e, put):
        es = swap_halves(e)

        def body(i, c):
            for k in range(chunk):
                u = i * chunk + k
                h = h_ref[u]
                m, q = h * e, h * es
                m = sum(m[:, 128 * t : 128 * t + 128] for t in range(tiles))
                q = sum(q[:, 128 * t : 128 * t + 128] for t in range(tiles))
                v = jnp.where(top, m + swap_halves(m), swap_halves(q) - q)
                put(u, jnp.broadcast_to(jnp.sum(v, 1, keepdims=True), (8, 128)))
            return c

        lax.fori_loop(0, users // chunk, body, 0)

    y = forward(lambda u: s_ref[u]) + n_ref[...]
    errs = []
    for layer in range(LAYERS):
        e = y if layer == 0 else y - forward(lambda u: xs_ref[layer, u])
        errs.append(e)
        step = s_ref[users + layer]

        def put(u, v):
            z = step * v if layer == 0 else xs_ref[layer, u] + step * v
            xs_ref[layer + 1, u] = clip_level * jnp.tanh(z * (1.0 / clip_level))

        adjoint(e, put)

    x_out_ref[...] = xs_ref[LAYERS]
    backs = [None] * LAYERS
    for layer in reversed(range(LAYERS)):
        step = s_ref[users + layer]
        last = layer == LAYERS - 1

        def slope(i, c):
            for k in range(chunk):
                u = i * chunk + k
                x = xs_ref[layer + 1, u]
                gx = (x - s_ref[u]) * (2.0 / users) if last else gx_ref[u]
                t = x * (1.0 / clip_level)
                gz_ref[layer, u] = gx * (1.0 - t * t) * step
            return c

        lax.fori_loop(0, users // chunk, slope, 0)
        ge = forward(lambda u: gz_ref[layer, u])
        backs[layer] = ge
        if layer:
            def put(u, v):
                x = xs_ref[layer + 1, u]
                gx = (x - s_ref[u]) * (2.0 / users) if last else gx_ref[u]
                t = x * (1.0 / clip_level)
                gx_ref[u] = gx * (1.0 - t * t) - v

            adjoint(ge, put)

    sign = half_rows((8, ant), 0, 1.0, -1.0)
    pairs = [(v, sign * swap_halves(v)) for k in range(LAYERS) for v in (errs[k], backs[k])]

    def outer(u):
        s = s_ref[u]
        g = jnp.zeros((8, ant), jnp.float32)
        for k in range(LAYERS):
            for which in range(2):
                v, vs = pairs[2 * k + which]
                if which == 0:
                    b = gz_ref[k, u]
                else:
                    b = s - xs_ref[k, u] if k else s
                bs = swap_halves(b)
                g = g + v * wide(jnp.where(top, b, bs)) + vs * wide(jnp.where(top, bs, b))
        g_ref[u] = g

    def body(i, c):
        for k in range(16):
            outer(i * 16 + k)
        return c

    lax.fori_loop(0, users // 16, body, 0)


def detect(channel, symbols, noise):
    users, _, ant = channel.shape
    return pl.pallas_call(
        functools.partial(detect_kernel, users),
        in_specs=[
            pl.BlockSpec(memory_space=pltpu.VMEM),
            pl.BlockSpec(memory_space=pltpu.VMEM),
            pl.BlockSpec(memory_space=pltpu.VMEM),
        ],
        out_specs=[pl.BlockSpec(memory_space=pltpu.VMEM), pl.BlockSpec(memory_space=pltpu.VMEM)],
        out_shape=[
            jax.ShapeDtypeStruct((users, 8, ant), jnp.float32),
            jax.ShapeDtypeStruct((users, 8, 128), jnp.float32),
        ],
        scratch_shapes=[
            pltpu.VMEM((LAYERS + 1, users, 8, 128), jnp.float32),
            pltpu.VMEM((LAYERS, users, 8, 128), jnp.float32),
            pltpu.VMEM((users, 8, 128), jnp.float32),
        ],
        compiler_params=pltpu.CompilerParams(vmem_limit_bytes=16 << 20),
        name="detect",
    )(channel, symbols, noise)


def grad_kernel(n, ul, pw, per, unroll, g_ref, e_ref, x_ref, out_ref, w_ref, lhs_ref, mat_ref):
    u = pl.program_id(0)
    step = pl.program_id(1)
    parts = pw // 128
    ant = g_ref.shape[-1]
    half = ant // 2
    rows = lhs_ref.shape[0]

    @pl.when((u == 0) & (step == 0))
    def _():
        mat_ref[...] = jnp.zeros_like(mat_ref)

    @pl.when(step == 0)
    def _():
        plus = g_ref[:, u, :, pl.ds(0, half)]
        minus = g_ref[:, u, :, pl.ds(half, half)]
        odd = swap_halves(plus - minus) * half_rows(plus.shape, 1, -1.0, 1.0)
        mix = jnp.concatenate([plus + minus, odd], 2).reshape(rows, ant)
        high, low = split(mix)
        lhs_ref[:, pl.ds(0, ant)] = high
        lhs_ref[:, pl.ds(ant, ant)] = low

    sign = half_rows((8, pw), 0, 1.0, -1.0)
    kinds = lax.broadcasted_iota(jnp.int32, (MAT, pw), 0).astype(jnp.float32)

    def tile(i, slot):
        s = step * per + i
        fine = e_ref[0, i, pl.ds(rows, 16), :]
        coarse = e_ref[0, i, pl.ds(rows + 16, ant // 16), :]
        steering(fine, coarse, w_ref, slot)
        w_high = w_ref[slot, pl.ds(0, ant), :]
        w_low = w_ref[slot, pl.ds(ant, ant), :]
        l_high = lhs_ref[:, pl.ds(0, ant)]
        left = jnp.concatenate([l_high, lhs_ref[:, pl.ds(ant, ant)]], 0)
        pair = jnp.dot(left, w_high, preferred_element_type=jnp.float32)
        rest = jnp.dot(l_high, w_low, preferred_element_type=jnp.float32)
        q = (pair[:rows] + (pair[rows:] + rest)).reshape(rows // 8, 8, pw)
        e = e_ref[0, i, pl.ds(0, rows), :].reshape(rows // 8, 8, pw)
        a = jnp.sum(e * q, 0)
        b = jnp.sum(swap_halves(e) * q, 0)
        p_re = jnp.sum(a * sign, 0, keepdims=True)
        p_im = jnp.sum(b, 0, keepdims=True)
        for t in range(parts):
            lanes = slice(128 * t, 128 * t + 128)
            out_ref[s, t * ul + u] = p_re[:, lanes]
            out_ref[s, (parts + t) * ul + u] = p_im[:, lanes]
        g_re, g_im, mat = (field_row(x_ref, parts, ul, s, j, u) for j in (2, 3, 4))
        along_re = g_re * p_re + g_im * p_im
        along_im = g_re * p_im - g_im * p_re
        hit = jnp.broadcast_to(mat, (MAT, pw)) == kinds
        mat_ref[0] += jnp.where(hit, jnp.broadcast_to(along_re, (MAT, pw)), 0.0)
        mat_ref[1] += jnp.where(hit, jnp.broadcast_to(along_im, (MAT, pw)), 0.0)

    def group(i, carry):
        for slot in range(unroll):
            tile(i * unroll + slot, slot)
        return carry

    lax.fori_loop(0, per // unroll, group, 0)

    @pl.when((u == ul - 1) & (step == n // per - 1))
    def _():
        lane = lax.broadcasted_iota(jnp.int32, (MAT, 128), 1)
        kind = lax.broadcasted_iota(jnp.int32, (MAT, 128), 0)
        line = jnp.zeros((1, 128), jnp.float32)
        for j in range(2):
            total = jnp.broadcast_to(jnp.sum(mat_ref[j], 1, keepdims=True), (MAT, 128))
            spread = jnp.where(lane == kind + j * MAT, total, 0.0)
            line = line + jnp.sum(spread, 0, keepdims=True)
        for s in range(n):
            out_ref[s, 2 * parts * ul] = line


def gradient(grads, kept, params):
    n, ul, _, ant = grads.shape
    pw = kept.shape[-1]
    rows = 8 * n
    sent = 2 * ul * (pw // 128) + 1
    per = n // GRAD_STEPS if n % GRAD_STEPS == 0 else n
    unroll = math.gcd(per, GRAD_UNROLL)
    return pl.pallas_call(
        functools.partial(grad_kernel, n, ul, pw, per, unroll),
        grid=(ul, n // per),
        in_specs=[
            pl.BlockSpec(memory_space=pltpu.VMEM),
            pl.BlockSpec((1, per, kept.shape[2], pw), lambda u, j: (u, j, 0, 0)),
            pl.BlockSpec(memory_space=pltpu.VMEM),
        ],
        out_specs=pl.BlockSpec((n, sent, 1, 128), lambda u, j: (0, 0, 0, 0)),
        out_shape=jax.ShapeDtypeStruct((n, sent, 1, 128), jnp.float32),
        scratch_shapes=[
            pltpu.VMEM((unroll, 2 * ant, pw), jnp.bfloat16),
            pltpu.VMEM((rows, 2 * ant), jnp.bfloat16),
            pltpu.VMEM((2, MAT, pw), jnp.float32),
        ],
        compiler_params=pltpu.CompilerParams(vmem_limit_bytes=GRAD_VMEM),
        name="gradient",
    )(grads, kept, params)


def unpack_kernel(n, ul, x_ref, grad_ref, mat_ref):
    parts = grad_ref.shape[-1] // 128
    total = x_ref[0, 2 * parts * ul]
    for s in range(1, n):
        total = total + x_ref[s, 2 * parts * ul]
    for j in range(2):
        mat_ref[pl.ds(j, 1), :] = total[:, j * MAT : j * MAT + MAT]
    for s in range(n):
        for j in range(2):
            for t in range(parts):
                rows = [x_ref[s, (j * parts + t) * ul + k] for k in range(ul)]
                rows = jnp.concatenate(rows, 0)
                grad_ref[j, pl.ds(s * ul, ul), pl.ds(128 * t, 128)] = rows


def unpack(received, users, pw):
    n = received.shape[0]
    return pl.pallas_call(
        functools.partial(unpack_kernel, n, users // n),
        in_specs=[pl.BlockSpec(memory_space=pltpu.VMEM)],
        out_specs=[pl.BlockSpec(memory_space=pltpu.VMEM)] * 2,
        out_shape=[
            jax.ShapeDtypeStruct((2, users, pw), jnp.float32),
            jax.ShapeDtypeStruct((2, MAT), jnp.float32),
        ],
        compiler_params=pltpu.CompilerParams(vmem_limit_bytes=8 << 20),
        name="unpack",
    )(received)


def antenna_order(ant):
    half = ant // 2
    offset = np.arange(half).reshape(-1, 2, 8)
    offset = np.stack([offset[:, 1], offset[:, 0, ::-1]], 1).reshape(half)
    return np.concatenate([half + offset, half - 1 - offset])


def exchange(x):
    return lax.all_to_all(x, "path", 0, 0, tiled=True)


def local(
    n,
    path_angle,
    path_delay,
    path_gain,
    material_ids,
    reflection,
    step_sizes,
    tone_ids,
    symbol_ids,
    receiver_noise,
):
    users, pw = path_angle.shape
    own, _, ant = receiver_noise.shape
    assert 2 * own == 8
    ul = users // n
    params = exchange(pack(n, path_angle, path_delay, path_gain, material_ids))
    tone = tone_ids.astype(jnp.float32) * (1.0 / TONE_SPAN)
    tone = jnp.broadcast_to(tone.reshape(n, 1, own), (n, 2, own)).reshape(8 * n)
    aux = jnp.concatenate([tone, reflection.reshape(2 * MAT)])
    aux = jnp.broadcast_to(aux[:, None], (8 * n + 2 * MAT, 128))
    channel_rows, kept = synthesize(params, aux, ul, pw, ant)
    channel = exchange(channel_rows).reshape(users, 8, ant)

    symbols = jnp.stack([symbol_ids % 4, symbol_ids // 4], 0)
    symbols = (2 * symbols - 3).astype(jnp.float32) * qam_scale
    symbols = jnp.transpose(symbols, (2, 0, 1)).reshape(users, 8)
    symbols = jnp.concatenate([symbols, jnp.broadcast_to(step_sizes[:, None], (LAYERS, 8))], 0)
    symbols = jnp.broadcast_to(symbols[:, :, None], (users + LAYERS, 8, 128))
    noise = jnp.transpose(receiver_noise, (1, 0, 2)).reshape(8, ant)
    order = jnp.asarray(antenna_order(ant), jnp.int32)
    place = (order[None] == jnp.arange(ant, dtype=jnp.int32)[:, None]).astype(jnp.float32)
    noise = jnp.dot(noise, place, precision=lax.Precision.HIGHEST)
    grads, found = detect(channel, symbols, noise)
    estimates = jnp.transpose(found[:, :, 0].reshape(users, 2, own), (2, 1, 0))

    grads = exchange(grads.reshape(n, ul, 8, ant))
    sent = gradient(grads, kept, params)
    back = exchange(sent)
    path_grad, material_grad = unpack(back, users, pw)

    responses = jnp.transpose(channel.reshape(users, 2, own, ant), (2, 1, 0, 3))
    responses = jnp.einsum("...k,ak->...a", responses, place, precision=lax.Precision.HIGHEST)
    return (path_grad, estimates, material_grad, responses)


def solution(mesh):
    in_specs = (
        P(None, ("groups", "path")),
        P(None, ("groups", "path")),
        P(None, None, ("groups", "path")),
        P(None, ("groups", "path")),
        P(),
        P(),
        P("groups"),
        P(("groups", "path"), None),
        P(("groups", "path"), None, None),
    )
    out_specs = (
        P(None, None, ("groups", "path")),
        P(("groups", "path"), None, None),
        P(None, "groups"),
        P(("groups", "path"), None, None, None),
    )
    body = functools.partial(local, mesh.shape["path"])
    return jax.shard_map(body, mesh=mesh, in_specs=in_specs, out_specs=out_specs, check_vma=False)
```

```python
import functools
import math

import jax
import jax.numpy as jnp
import numpy as np
from jax import lax
from jax.experimental import pallas as pl
from jax.experimental.pallas import tpu as pltpu
from jax.sharding import PartitionSpec as P

MAT = 16
TONE_SPAN = 3276
LAYERS = 4
FIELDS = 5

SYNTH_VMEM = 48 << 20
GRAD_VMEM = 48 << 20
SYNTH_UNROLL = 16
SYNTH_JOINED = 16
GRAD_UNROLL = 8
DETECT_UNROLL = 64
GRAD_STEPS = 1

clip_level = 1.5
qam_scale = 1.0 / math.sqrt(10.0)

SINE = (
    6.283185160088971,
    -41.341655031286386,
    81.60100406453228,
    -76.5497820808334,
    39.536704364112744,
)


def cos_turns(t):
    a = 0.25 - jnp.abs(t - jnp.round(t))
    z = a * a
    p = SINE[4] * z + SINE[3]
    p = p * z + SINE[2]
    p = p * z + SINE[1]
    p = p * z + SINE[0]
    return p * a


RISE = (
    -0.16666660462354993,
    0.00833308816681783,
    -0.00019811112712181806,
    2.6089325665533767e-06,
)


def sine(angle):
    t = jnp.abs(angle)
    y = jnp.where(t > 0.5 * math.pi, (3.140625 - t) + (math.pi - 3.140625), t)
    z = y * y
    p = RISE[3] * z + RISE[2]
    p = p * z + RISE[1]
    p = p * z + RISE[0]
    s = y + (y * z) * p
    return jnp.where(angle < 0.0, -s, s)


def swap_halves(x):
    return pltpu.roll(x, 4, x.ndim - 2)


def half_rows(shape, dim, top, bottom):
    row = lax.broadcasted_iota(jnp.int32, shape, dim)
    return jnp.where(row % 8 < 4, jnp.float32(top), jnp.float32(bottom))


def top_mask(shape, dim):
    return lax.broadcasted_iota(jnp.int32, shape, dim) % 8 < 4


def split(x):
    high = x.astype(jnp.bfloat16)
    low = (x - high.astype(jnp.float32)).astype(jnp.bfloat16)
    return high, low


def pack_kernel(n, ul, angle_ref, delay_ref, gain_ref, ids_ref, out_ref):
    pw = angle_ref.shape[-1]
    fields = (
        0.5 * sine(angle_ref[...]),
        delay_ref[...],
        gain_ref[0],
        gain_ref[1],
        ids_ref[...].astype(jnp.float32),
    )
    parts = pw // 128
    for j, field in enumerate(fields):
        for t in range(parts):
            block = field[:, 128 * t : 128 * t + 128]
            for d in range(n):
                start = (j * parts + t) * ul
                out_ref[d, pl.ds(start, ul), :] = block[d * ul : d * ul + ul]


def pack(n, angle, delay, gain, ids):
    users, pw = angle.shape
    ul = users // n
    rows = FIELDS * ul * (pw // 128)
    return pl.pallas_call(
        functools.partial(pack_kernel, n, ul),
        in_specs=[pl.BlockSpec(memory_space=pltpu.VMEM)] * 4,
        out_specs=pl.BlockSpec(memory_space=pltpu.VMEM),
        out_shape=jax.ShapeDtypeStruct((n, rows, 128), jnp.float32),
        compiler_params=pltpu.CompilerParams(vmem_limit_bytes=60 << 20),
        name="pack",
    )(angle, delay, gain, ids)


def field_row(x_ref, parts, ul, s, j, u):
    rows = [x_ref[s, pl.ds((j * parts + t) * ul + u, 1), :] for t in range(parts)]
    return jnp.concatenate(rows, 1)


def steering(fine, coarse, w_ref, slot):
    blocks = coarse.shape[0] // 2
    half = 16 * blocks
    f_cos, f_sin = fine[:8], fine[8:]
    for b in range(blocks):
        c_cos = coarse[b : b + 1]
        c_sin = coarse[blocks + b : blocks + b + 1]
        cc, ss = c_cos * f_cos, c_sin * f_sin
        sc, cs = c_sin * f_cos, c_cos * f_sin
        a_cos = jnp.concatenate([cc - ss, cc + ss], 0)
        a_sin = jnp.concatenate([sc + cs, sc - cs], 0)
        for base, val in ((0, a_cos), (half, a_sin)):
            high, low = split(val)
            w_ref[slot, pl.ds(base + 16 * b, 16), :] = high
            w_ref[slot, pl.ds(2 * half + base + 16 * b, 16), :] = low


def synth_kernel(n, ul, pw, unroll, x_ref, aux_ref, h_ref, e_ref, w_ref, lhs_ref, acc_ref, c_ref):
    u = pl.program_id(0)
    parts = pw // 128
    half = acc_ref.shape[-1] // 2
    rows = acc_ref.shape[0]
    top8 = top_mask((8, pw), 0)
    shift8 = half_rows((8, pw), 0, 0.0, -0.25)
    blocks = half // 16
    fine_row = lax.broadcasted_iota(jnp.int32, (16, pw), 0)
    fine_coef = (fine_row % 8).astype(jnp.float32) + 0.5
    fine_shift = jnp.where(fine_row < 8, 0.0, -0.25)
    coarse_row = lax.broadcasted_iota(jnp.int32, (2 * blocks, pw), 0)
    coarse_coef = (coarse_row % blocks).astype(jnp.float32) * 16.0 + 8.0
    coarse_shift = jnp.where(coarse_row < blocks, 0.0, -0.25)

    def coefficients():
        def column(j):
            return jnp.concatenate([field_row(x_ref, parts, ul, s, j, u) for s in range(n)], 0)

        def wide(r):
            line = jnp.broadcast_to(aux_ref[pl.ds(rows + r, 1), :], (n, 128))
            return jnp.concatenate([line] * parts, 1)

        g_re, g_im, mat = (column(j) for j in (2, 3, 4))
        mat = mat.astype(jnp.int32)
        bits = [(mat & (1 << bit)) != 0 for bit in range(MAT.bit_length() - 1)]
        refl = []
        for base in (0, MAT):
            level = [wide(base + m) for m in range(MAT)]
            for hit in bits:
                level = [jnp.where(hit, y, x) for x, y in zip(level[::2], level[1::2])]
            refl.append(level[0])
        c_ref[0] = g_re * refl[0] - g_im * refl[1]
        c_ref[1] = g_re * refl[1] + g_im * refl[0]

    def tile(s, slot):
        w, dly = (field_row(x_ref, parts, ul, s, j, u) for j in range(2))
        w8 = jnp.broadcast_to(w, (8, pw))
        fine = cos_turns(fine_coef * jnp.concatenate([w8] * 2, 0) + fine_shift)
        w16 = jnp.concatenate([w8] * (2 * blocks // 8), 0)
        coarse = cos_turns(coarse_coef * w16 + coarse_shift)
        e_ref[0, s, pl.ds(rows, 16), :] = fine
        e_ref[0, s, pl.ds(rows + 16, 2 * blocks), :] = coarse
        steering(fine, coarse, w_ref, slot)
        c_re = jnp.broadcast_to(c_ref[0, pl.ds(s, 1), :], (8, pw))
        c_im = jnp.broadcast_to(c_ref[1, pl.ds(s, 1), :], (8, pw))
        c_mix = jnp.where(top8, c_re, -c_re)
        centre = w * (half - 0.5)
        centre = centre - jnp.round(centre)
        base8 = shift8 + centre
        d8 = jnp.broadcast_to(dly, (8, pw))
        step = 32
        for q in range(rows // step):
            rq = pl.ds(q * step, step)
            tone = aux_ref[rq, :]
            tone = jnp.concatenate([tone] * parts, 1)
            d32 = jnp.concatenate([d8] * (step // 8), 0)
            b32 = jnp.concatenate([base8] * (step // 8), 0)
            e = cos_turns(tone * d32 + b32)
            e_ref[0, s, rq, :] = e
            e3 = e.reshape(step // 8, 8, pw)
            g = e3 * c_mix[None] + swap_halves(e3) * c_im[None]
            high, low = split(g.reshape(step, pw))
            lhs_ref[slot, rq, pl.ds(0, pw)] = high
            lhs_ref[slot, rq, pl.ds(pw, pw)] = low

    def product(slots):
        def lhs(base):
            return jnp.concatenate([lhs_ref[k, :, pl.ds(base, pw)] for k in slots], 1)

        def steer(base):
            return jnp.concatenate([w_ref[k, pl.ds(base, 2 * half), :] for k in slots], 1)

        dims = (((1,), (1,)), ((), ()))
        l_high = lhs(0)
        left = jnp.concatenate([l_high, lhs(pw)], 0)
        pair = lax.dot_general(left, steer(0), dims, preferred_element_type=jnp.float32)
        rest = lax.dot_general(l_high, steer(2 * half), dims, preferred_element_type=jnp.float32)
        acc_ref[...] += pair[:rows] + (pair[rows:] + rest)

    joined = math.gcd(unroll, SYNTH_JOINED)

    def group(i, carry):
        for first in range(0, unroll, joined):
            slots = range(first, first + joined)
            for slot in slots:
                tile(i * unroll + slot, slot)
            product(slots)
        return carry

    coefficients()
    acc_ref[...] = jnp.zeros_like(acc_ref)
    lax.fori_loop(0, n // unroll, group, 0)
    even = acc_ref[:, pl.ds(0, half)].reshape(rows // 8, 8, half)
    odd = acc_ref[:, pl.ds(half, half)].reshape(rows // 8, 8, half)
    odd = swap_halves(odd) * half_rows(odd.shape, 1, 1.0, -1.0)
    h_ref[:, 0, :, pl.ds(0, half)] = even + odd
    h_ref[:, 0, :, pl.ds(half, half)] = even - odd


def synthesize(params, aux, ul, pw, antennas):
    n = params.shape[0]
    rows = 8 * n
    kept = rows + 16 + antennas // 16
    unroll = math.gcd(n, SYNTH_UNROLL)
    return pl.pallas_call(
        functools.partial(synth_kernel, n, ul, pw, unroll),
        grid=(ul,),
        in_specs=[
            pl.BlockSpec(memory_space=pltpu.VMEM),
            pl.BlockSpec(memory_space=pltpu.VMEM),
        ],
        out_specs=[
            pl.BlockSpec((n, 1, 8, antennas), lambda u: (0, u, 0, 0)),
            pl.BlockSpec((1, n, kept, pw), lambda u: (u, 0, 0, 0)),
        ],
        out_shape=[
            jax.ShapeDtypeStruct((n, ul, 8, antennas), jnp.float32),
            jax.ShapeDtypeStruct((ul, n, kept, pw), jnp.float32),
        ],
        scratch_shapes=[
            pltpu.VMEM((unroll, 2 * antennas, pw), jnp.bfloat16),
            pltpu.VMEM((unroll, rows, 2 * pw), jnp.bfloat16),
            pltpu.VMEM((rows, antennas), jnp.float32),
            pltpu.VMEM((2, n, pw), jnp.float32),
        ],
        compiler_params=pltpu.CompilerParams(vmem_limit_bytes=SYNTH_VMEM),
        name="synth",
    )(params, aux)


def detect_kernel(users, h_ref, s_ref, n_ref, g_ref, x_out_ref, xs_ref, gz_ref, gx_ref):
    ant = h_ref.shape[-1]
    tiles = ant // 128
    top = top_mask((8, 128), 0)
    top_a = top_mask((8, ant), 0)
    chunk = DETECT_UNROLL

    def wide(x):
        return jnp.concatenate([x] * tiles, 1) if tiles > 1 else x

    def forward(get):
        def body(i, c):
            c = list(c)
            for k in range(chunk):
                u = i * chunk + k
                h = h_ref[u]
                x = get(u)
                j = 2 * (k % 4)
                c[j] = c[j] + h * wide(x)
                c[j + 1] = c[j + 1] + h * wide(swap_halves(x))
            return tuple(c)

        zero = jnp.zeros((8, ant), jnp.float32)
        c = lax.fori_loop(0, users // chunk, body, (zero,) * 8)
        a = (c[0] + c[2]) + (c[4] + c[6])
        b = (c[1] + c[3]) + (c[5] + c[7])
        return jnp.where(top_a, a - swap_halves(a), b + swap_halves(b))

    def adjoint(e, put):
        es = swap_halves(e)

        def body(i, c):
            for k in range(chunk):
                u = i * chunk + k
                h = h_ref[u]
                m, q = h * e, h * es
                m = sum(m[:, 128 * t : 128 * t + 128] for t in range(tiles))
                q = sum(q[:, 128 * t : 128 * t + 128] for t in range(tiles))
                v = jnp.where(top, m + swap_halves(m), swap_halves(q) - q)
                put(u, jnp.broadcast_to(jnp.sum(v, 1, keepdims=True), (8, 128)))
            return c

        lax.fori_loop(0, users // chunk, body, 0)

    y = forward(lambda u: s_ref[u]) + n_ref[...]
    errs = []
    for layer in range(LAYERS):
        e = y if layer == 0 else y - forward(lambda u: xs_ref[layer, u])
        errs.append(e)
        step = s_ref[users + layer]

        def put(u, v):
            z = step * v if layer == 0 else xs_ref[layer, u] + step * v
            xs_ref[layer + 1, u] = clip_level * jnp.tanh(z * (1.0 / clip_level))

        adjoint(e, put)

    x_out_ref[...] = xs_ref[LAYERS]
    backs = [None] * LAYERS
    for layer in reversed(range(LAYERS)):
        step = s_ref[users + layer]
        last = layer == LAYERS - 1

        def slope(i, c):
            for k in range(chunk):
                u = i * chunk + k
                x = xs_ref[layer + 1, u]
                gx = (x - s_ref[u]) * (2.0 / users) if last else gx_ref[u]
                t = x * (1.0 / clip_level)
                gz_ref[layer, u] = gx * (1.0 - t * t) * step
            return c

        lax.fori_loop(0, users // chunk, slope, 0)
        ge = forward(lambda u: gz_ref[layer, u])
        backs[layer] = ge
        if layer:
            def put(u, v):
                x = xs_ref[layer + 1, u]
                gx = (x - s_ref[u]) * (2.0 / users) if last else gx_ref[u]
                t = x * (1.0 / clip_level)
                gx_ref[u] = gx * (1.0 - t * t) - v

            adjoint(ge, put)

    sign = half_rows((8, ant), 0, 1.0, -1.0)
    pairs = [(v, sign * swap_halves(v)) for k in range(LAYERS) for v in (errs[k], backs[k])]

    def outer(u):
        s = s_ref[u]
        g = jnp.zeros((8, ant), jnp.float32)
        for k in range(LAYERS):
            for which in range(2):
                v, vs = pairs[2 * k + which]
                if which == 0:
                    b = gz_ref[k, u]
                else:
                    b = s - xs_ref[k, u] if k else s
                bs = swap_halves(b)
                g = g + v * wide(jnp.where(top, b, bs)) + vs * wide(jnp.where(top, bs, b))
        g_ref[u] = g

    def body(i, c):
        for k in range(16):
            outer(i * 16 + k)
        return c

    lax.fori_loop(0, users // 16, body, 0)


def detect(channel, symbols, noise):
    users, _, ant = channel.shape
    return pl.pallas_call(
        functools.partial(detect_kernel, users),
        in_specs=[
            pl.BlockSpec(memory_space=pltpu.VMEM),
            pl.BlockSpec(memory_space=pltpu.VMEM),
            pl.BlockSpec(memory_space=pltpu.VMEM),
        ],
        out_specs=[pl.BlockSpec(memory_space=pltpu.VMEM), pl.BlockSpec(memory_space=pltpu.VMEM)],
        out_shape=[
            jax.ShapeDtypeStruct((users, 8, ant), jnp.float32),
            jax.ShapeDtypeStruct((users, 8, 128), jnp.float32),
        ],
        scratch_shapes=[
            pltpu.VMEM((LAYERS + 1, users, 8, 128), jnp.float32),
            pltpu.VMEM((LAYERS, users, 8, 128), jnp.float32),
            pltpu.VMEM((users, 8, 128), jnp.float32),
        ],
        compiler_params=pltpu.CompilerParams(vmem_limit_bytes=16 << 20),
        name="detect",
    )(channel, symbols, noise)


def grad_kernel(n, ul, pw, per, unroll, g_ref, e_ref, x_ref, out_ref, w_ref, lhs_ref, mat_ref):
    u = pl.program_id(0)
    step = pl.program_id(1)
    parts = pw // 128
    ant = g_ref.shape[-1]
    half = ant // 2
    rows = lhs_ref.shape[0]

    @pl.when((u == 0) & (step == 0))
    def _():
        mat_ref[...] = jnp.zeros_like(mat_ref)

    @pl.when(step == 0)
    def _():
        plus = g_ref[:, u, :, pl.ds(0, half)]
        minus = g_ref[:, u, :, pl.ds(half, half)]
        odd = swap_halves(plus - minus) * half_rows(plus.shape, 1, -1.0, 1.0)
        mix = jnp.concatenate([plus + minus, odd], 2).reshape(rows, ant)
        high, low = split(mix)
        lhs_ref[:, pl.ds(0, ant)] = high
        lhs_ref[:, pl.ds(ant, ant)] = low

    sign = half_rows((8, pw), 0, 1.0, -1.0)
    kinds = lax.broadcasted_iota(jnp.int32, (MAT, pw), 0).astype(jnp.float32)

    def tile(i, slot):
        s = step * per + i
        fine = e_ref[0, i, pl.ds(rows, 16), :]
        coarse = e_ref[0, i, pl.ds(rows + 16, ant // 16), :]
        steering(fine, coarse, w_ref, slot)
        w_high = w_ref[slot, pl.ds(0, ant), :]
        w_low = w_ref[slot, pl.ds(ant, ant), :]
        l_high = lhs_ref[:, pl.ds(0, ant)]
        left = jnp.concatenate([l_high, lhs_ref[:, pl.ds(ant, ant)]], 0)
        pair = jnp.dot(left, w_high, preferred_element_type=jnp.float32)
        rest = jnp.dot(l_high, w_low, preferred_element_type=jnp.float32)
        q = (pair[:rows] + (pair[rows:] + rest)).reshape(rows // 8, 8, pw)
        e = e_ref[0, i, pl.ds(0, rows), :].reshape(rows // 8, 8, pw)
        a = jnp.sum(e * q, 0)
        b = jnp.sum(swap_halves(e) * q, 0)
        p_re = jnp.sum(a * sign, 0, keepdims=True)
        p_im = jnp.sum(b, 0, keepdims=True)
        for t in range(parts):
            lanes = slice(128 * t, 128 * t + 128)
            out_ref[s, t * ul + u] = p_re[:, lanes]
            out_ref[s, (parts + t) * ul + u] = p_im[:, lanes]
        g_re, g_im, mat = (field_row(x_ref, parts, ul, s, j, u) for j in (2, 3, 4))
        along_re = g_re * p_re + g_im * p_im
        along_im = g_re * p_im - g_im * p_re
        hit = jnp.broadcast_to(mat, (MAT, pw)) == kinds
        mat_ref[0] += jnp.where(hit, jnp.broadcast_to(along_re, (MAT, pw)), 0.0)
        mat_ref[1] += jnp.where(hit, jnp.broadcast_to(along_im, (MAT, pw)), 0.0)

    def group(i, carry):
        for slot in range(unroll):
            tile(i * unroll + slot, slot)
        return carry

    lax.fori_loop(0, per // unroll, group, 0)

    @pl.when((u == ul - 1) & (step == n // per - 1))
    def _():
        lane = lax.broadcasted_iota(jnp.int32, (MAT, 128), 1)
        kind = lax.broadcasted_iota(jnp.int32, (MAT, 128), 0)
        line = jnp.zeros((1, 128), jnp.float32)
        for j in range(2):
            total = jnp.broadcast_to(jnp.sum(mat_ref[j], 1, keepdims=True), (MAT, 128))
            spread = jnp.where(lane == kind + j * MAT, total, 0.0)
            line = line + jnp.sum(spread, 0, keepdims=True)
        for s in range(n):
            out_ref[s, 2 * parts * ul] = line


def gradient(grads, kept, params):
    n, ul, _, ant = grads.shape
    pw = kept.shape[-1]
    rows = 8 * n
    sent = 2 * ul * (pw // 128) + 1
    per = n // GRAD_STEPS if n % GRAD_STEPS == 0 else n
    unroll = math.gcd(per, GRAD_UNROLL)
    return pl.pallas_call(
        functools.partial(grad_kernel, n, ul, pw, per, unroll),
        grid=(ul, n // per),
        in_specs=[
            pl.BlockSpec(memory_space=pltpu.VMEM),
            pl.BlockSpec((1, per, kept.shape[2], pw), lambda u, j: (u, j, 0, 0)),
            pl.BlockSpec(memory_space=pltpu.VMEM),
        ],
        out_specs=pl.BlockSpec((n, sent, 1, 128), lambda u, j: (0, 0, 0, 0)),
        out_shape=jax.ShapeDtypeStruct((n, sent, 1, 128), jnp.float32),
        scratch_shapes=[
            pltpu.VMEM((unroll, 2 * ant, pw), jnp.bfloat16),
            pltpu.VMEM((rows, 2 * ant), jnp.bfloat16),
            pltpu.VMEM((2, MAT, pw), jnp.float32),
        ],
        compiler_params=pltpu.CompilerParams(vmem_limit_bytes=GRAD_VMEM),
        name="gradient",
    )(grads, kept, params)


def unpack_kernel(n, ul, x_ref, grad_ref, mat_ref):
    parts = grad_ref.shape[-1] // 128
    total = x_ref[0, 2 * parts * ul]
    for s in range(1, n):
        total = total + x_ref[s, 2 * parts * ul]
    for j in range(2):
        mat_ref[pl.ds(j, 1), :] = total[:, j * MAT : j * MAT + MAT]
    for s in range(n):
        for j in range(2):
            for t in range(parts):
                rows = [x_ref[s, (j * parts + t) * ul + k] for k in range(ul)]
                rows = jnp.concatenate(rows, 0)
                grad_ref[j, pl.ds(s * ul, ul), pl.ds(128 * t, 128)] = rows


def unpack(received, users, pw):
    n = received.shape[0]
    return pl.pallas_call(
        functools.partial(unpack_kernel, n, users // n),
        in_specs=[pl.BlockSpec(memory_space=pltpu.VMEM)],
        out_specs=[pl.BlockSpec(memory_space=pltpu.VMEM)] * 2,
        out_shape=[
            jax.ShapeDtypeStruct((2, users, pw), jnp.float32),
            jax.ShapeDtypeStruct((2, MAT), jnp.float32),
        ],
        compiler_params=pltpu.CompilerParams(vmem_limit_bytes=8 << 20),
        name="unpack",
    )(received)


def antenna_order(ant):
    half = ant // 2
    offset = np.arange(half).reshape(-1, 2, 8)
    offset = np.stack([offset[:, 1], offset[:, 0, ::-1]], 1).reshape(half)
    return np.concatenate([half + offset, half - 1 - offset])


def exchange(x):
    return lax.all_to_all(x, "path", 0, 0, tiled=True)


def local(
    n,
    path_angle,
    path_delay,
    path_gain,
    material_ids,
    reflection,
    step_sizes,
    tone_ids,
    symbol_ids,
    receiver_noise,
):
    users, pw = path_angle.shape
    own, _, ant = receiver_noise.shape
    assert 2 * own == 8
    ul = users // n
    params = exchange(pack(n, path_angle, path_delay, path_gain, material_ids))
    tone = tone_ids.astype(jnp.float32) * (1.0 / TONE_SPAN)
    tone = jnp.broadcast_to(tone.reshape(n, 1, own), (n, 2, own)).reshape(8 * n)
    aux = jnp.concatenate([tone, reflection.reshape(2 * MAT)])
    aux = jnp.broadcast_to(aux[:, None], (8 * n + 2 * MAT, 128))
    channel_rows, kept = synthesize(params, aux, ul, pw, ant)
    channel = exchange(channel_rows).reshape(users, 8, ant)

    symbols = jnp.stack([symbol_ids % 4, symbol_ids // 4], 0)
    symbols = (2 * symbols - 3).astype(jnp.float32) * qam_scale
    symbols = jnp.transpose(symbols, (2, 0, 1)).reshape(users, 8)
    symbols = jnp.concatenate([symbols, jnp.broadcast_to(step_sizes[:, None], (LAYERS, 8))], 0)
    symbols = jnp.broadcast_to(symbols[:, :, None], (users + LAYERS, 8, 128))
    noise = jnp.transpose(receiver_noise, (1, 0, 2)).reshape(8, ant)
    order = jnp.asarray(antenna_order(ant), jnp.int32)
    place = (order[None] == jnp.arange(ant, dtype=jnp.int32)[:, None]).astype(jnp.float32)
    noise = jnp.dot(noise, place, precision=lax.Precision.HIGHEST)
    grads, found = detect(channel, symbols, noise)
    estimates = jnp.transpose(found[:, :, 0].reshape(users, 2, own), (2, 1, 0))

    grads = exchange(grads.reshape(n, ul, 8, ant))
    sent = gradient(grads, kept, params)
    back = exchange(sent)
    path_grad, material_grad = unpack(back, users, pw)

    responses = jnp.transpose(channel.reshape(users, 2, own, ant), (2, 1, 0, 3))
    responses = jnp.einsum("...k,ak->...a", responses, place, precision=lax.Precision.HIGHEST)
    return (path_grad, estimates, material_grad, responses)


def solution(mesh):
    in_specs = (
        P(None, ("groups", "path")),
        P(None, ("groups", "path")),
        P(None, None, ("groups", "path")),
        P(None, ("groups", "path")),
        P(),
        P(),
        P("groups"),
        P(("groups", "path"), None),
        P(("groups", "path"), None, None),
    )
    out_specs = (
        P(None, None, ("groups", "path")),
        P(("groups", "path"), None, None),
        P(None, "groups"),
        P(("groups", "path"), None, None, None),
    )
    body = functools.partial(local, mesh.shape["path"])
    return jax.shard_map(body, mesh=mesh, in_specs=in_specs, out_specs=out_specs, check_vma=False)
```
